32 devices in a mesh: groups: 2 (over x), along: 8 (over z, y), across: 2 (over core).
Axes of the slice: x: 2, y: 2, z: 4, core: 2. Of those that a mesh axis runs over, the one named last changes fastest.
Arguments:
- toa_bands: bfloat16 [1024, 4, 2048], P(('groups', 'along'), None, 'across'), parts along dimension 0, may hold values from 0.019897461 to 0.59765625
- dark_mask: int32 [1024, 2048], P(('groups', 'along'), 'across'), parts along dimension 0, may hold values 0 or 1
- vapour: float32 [1024, 2048], P(('groups', 'along'), 'across'), parts along dimension 0, may hold values from 0 to 7
- elev_class: int32 [1024, 2048], P(('groups', 'along'), 'across'), parts along dimension 0, may hold values from 0 to 6
- elev_frac: float32 [1024, 2048], P(('groups', 'along'), 'across'), parts along dimension 0, may hold values from 0 to 1
- kernel: float32 [61], replicated, may hold values from 0.1 to 1
- lut_gain: bfloat16 [4, 8, 16, 8], replicated, may hold values from 1 to 2
- lut_path: bfloat16 [4, 8, 16, 8], replicated, may hold values from 0 to 0.29882812
- lut_albedo: bfloat16 [4, 8, 16, 8], replicated, may hold values from 0.049804688 to 0.25
- routes: int32 [64, 2], P(('groups', 'along')), parts along dimension 0, may hold values from 0 to 7, as said below
- starts: int32 [64, 2], P(('groups', 'along')), parts along dimension 0, may hold values from 0 to 48
Outputs:
- tile_out: bfloat16 [16, 64, 4, 2048], P(('groups', 'along'), None, None, 'across'), parts along dimension 0
The draws below stay inside these ranges and needn't reach their ends.
There are 2 independent parts, one for each index of `groups`. The reference program is written for one: setup_inputs(seed, part) draws one part's arguments, and reference() takes and returns one part's arrays. A program takes and returns all parts, laid end to end along the dimension named above; an argument that names none is the same for every part. Nothing has to cross between parts.
Inputs may be any that keep to these rules, and one draw needn't show every extreme that they name: `dark_mask`: 1 marks a dark pixel. `elev_class`: the class and the next one are both classes of the table. `routes`: the first block of segment s is s // 4, the block of the segment's own rows; the second lies 1 to 2 blocks before or after it; among the 4 segments of one device at most 2 have their second block at any one signed distance, and in every draw some device has exactly 2 at some distance.
All inputs are finite; a program needn't handle non-finite values. No bound on the sum of `dark_mask` on one device may be relied on, other than what follows from the above.
Results may differ from the reference program's by a relative error of at most 0.0043.
Values may be sent and summed in bfloat16 or wider, within the bound.
A program may use at most 64 MiB of HBM per device.

```python
import math
import jax
import jax.numpy as jnp
from jax import lax

BANDS = 4
NA = 16
NW = 8
NE = 8
HALO = 30
SEG = 16
REACH = 2
ROW_DEV = 64
NR = 512
NC = 2048
SEG_DEV = 4
CAP = 2
NSEGS = 32
TILES = 8
TILE_ROWS = 64


def draw_routes(key, part):
    key_full = jax.random.fold_in(key, 101)
    key_slots = jax.random.fold_in(key, 202)
    key_order = jax.random.fold_in(key, 303)
    side_count = 2 * REACH
    side_ids = jnp.arange(side_count, dtype=jnp.int32)
    side_value = jnp.where(side_ids < REACH, side_ids - REACH, side_ids - REACH + 1)
    devices = jnp.arange(TILES, dtype=jnp.int32)
    dest = devices[:, None] + side_value[None, :]
    valid = (dest >= 0) & (dest < TILES)
    full_score = jax.random.randint(key_full, (TILES, side_count), 0, 1 << 16) * side_count + side_ids[None, :]
    full_side = jnp.argmax(jnp.where(valid, full_score, -1), axis=1).astype(jnp.int32)
    slot_ids = jnp.arange(side_count * CAP, dtype=jnp.int32)
    slot_side = slot_ids // CAP
    slot_score = jax.random.randint(key_slots, (TILES, side_count * CAP), 0, 1 << 16) * (side_count * CAP) + slot_ids[None, :]
    slot_valid = valid[:, slot_side]
    order_key = slot_score + (1 << 23) * (slot_side[None, :] != full_side[:, None]).astype(jnp.int32) + (1 << 25) * (1 - slot_valid.astype(jnp.int32))
    order = jnp.argsort(order_key, axis=1)[:, :SEG_DEV]
    chosen_side = slot_side[order]
    mix_score = jax.random.randint(key_order, (TILES, SEG_DEV), 0, 1 << 16) * SEG_DEV + jnp.arange(SEG_DEV, dtype=jnp.int32)[None, :]
    mix = jnp.argsort(mix_score, axis=1)
    chosen_side = jnp.take_along_axis(chosen_side, mix, axis=1)
    second = devices[:, None] + side_value[chosen_side]
    first = jnp.broadcast_to(devices[:, None], (TILES, SEG_DEV))
    return jnp.stack([first, second], axis=-1).reshape(NSEGS, 2).astype(jnp.int32)


def set_ends(entries, own_key, smallest, largest):
    shape = entries.shape
    index_at = [jax.random.randint(jax.random.fold_in(own_key, axis), (), 0, shape[axis]) for axis in range(len(shape))]
    entries = entries.at[tuple(index_at)].set(smallest)
    longest = shape.index(max(shape))
    index_at[longest] = (index_at[longest] + 1) % shape[longest]
    return entries.at[tuple(index_at)].set(largest)


def block_scale(rng, extent, split, least, top_value):
    gain = 1.0
    for position, parts in split:
        draws = jax.random.uniform(jax.random.fold_in(jax.random.fold_in(rng, 6), position), (parts,), jnp.float32, least / len(split), top_value / len(split))
        gain = gain * jnp.repeat(jnp.exp(draws), extent[position] // parts).reshape((-1,) + (1,) * (len(extent) - 1 - position))
    return gain


def setup_inputs(seed: int = 0, part: int = 0) -> dict:
    keys = jax.random.split(jax.random.key(seed), 12)
    part_splits = jax.random.split(jax.random.fold_in(keys[11], part), 12)
    return {
        "toa_bands": jnp.clip(0.019897461 + 0.5777588 * jax.random.uniform(part_splits[0], (NR, BANDS, NC), jnp.float32) ** block_scale(part_splits[0], (NR, BANDS, NC), ((0, 8), (2, 2)), -0.2, 0.2), 0.019897461, 0.59765625).astype(jnp.bfloat16),
        "dark_mask": set_ends((jax.random.randint(part_splits[1], (NR, NC), 0, 1024) < 1).astype(jnp.int32), jax.random.fold_in(part_splits[1], 1), 0, 1),
        "vapour": jnp.clip(7.0 * jax.random.uniform(part_splits[2], (NR, NC), jnp.float32) ** block_scale(part_splits[2], (NR, NC), ((0, 8), (1, 2)), -0.2, 0.2), 0.0, 7.0),
        "elev_class": set_ends(jax.random.randint(part_splits[3], (NR, NC), 0, NE - 1), jax.random.fold_in(part_splits[3], 1), 0, (NE - 1) - 1).astype(jnp.int32),
        "elev_frac": jnp.clip(1.0 * jax.random.uniform(part_splits[4], (NR, NC), jnp.float32) ** block_scale(part_splits[4], (NR, NC), ((0, 8), (1, 2)), -0.2, 0.2), 0.0, 1.0),
        "kernel": jnp.clip(jnp.exp(jax.random.uniform(keys[5], (2 * HALO + 1,), jnp.float32, math.log(0.1), math.log(1.0))), 0.1, 1.0),
        "lut_gain": jnp.clip(jax.random.uniform(keys[6], (BANDS, NE, NA, NW), jnp.float32, 1.0, 2.0), 1.0, 2.0).astype(jnp.bfloat16),
        "lut_path": jnp.clip(jax.random.uniform(keys[7], (BANDS, NE, NA, NW), jnp.float32, 0.0, 0.29882812), 0.0, 0.29882812).astype(jnp.bfloat16),
        "lut_albedo": jnp.clip(jax.random.uniform(keys[8], (BANDS, NE, NA, NW), jnp.float32, 0.049804688, 0.25), 0.049804688, 0.25).astype(jnp.bfloat16),
        "routes": draw_routes(jax.random.fold_in(jax.random.fold_in(keys[11], part), 71), part),
        "starts": set_ends(jax.random.randint(part_splits[10], (NSEGS, 2), 0, TILE_ROWS - SEG + 1), jax.random.fold_in(part_splits[10], 1), 0, TILE_ROWS - SEG).astype(jnp.int32),
    }


def smooth_axis(fields, kernel, axis):
    size = fields.shape[axis]
    tap_count = kernel.shape[0]
    half_width = tap_count // 2
    padding = [(0, 0), (0, 0), (0, 0)]
    padding[axis] = (half_width, half_width)
    padded = jnp.pad(fields, padding)
    total = jnp.zeros_like(fields)
    for tap in range(tap_count):
        total = total + kernel[tap] * lax.slice_in_dim(padded, tap, tap + size, axis=axis)
    return total


def correct_block(inputs, lut_table):
    toa_block, aero_pos, vapour_block, class_block, frac_block = inputs
    a_low = jnp.clip(jnp.floor(aero_pos).astype(jnp.int32), 0, NA - 2)
    a_frac = aero_pos - a_low.astype(aero_pos.dtype)
    w_low = jnp.clip(jnp.floor(vapour_block).astype(jnp.int32), 0, NW - 2)
    w_frac = vapour_block - w_low.astype(vapour_block.dtype)
    coefficient = jnp.zeros((lut_table.shape[0],) + aero_pos.shape, dtype=jnp.float32)
    for e_step in range(2):
        elev_weight = frac_block if e_step == 1 else 1.0 - frac_block
        for a_step in range(2):
            a_weight = a_frac if a_step == 1 else 1.0 - a_frac
            for w_step in range(2):
                w_weight = w_frac if w_step == 1 else 1.0 - w_frac
                joint_weight = (a_weight * w_weight).astype(jnp.bfloat16)
                joint_weight = lax.optimization_barrier(joint_weight).astype(jnp.float32)
                flat_index = ((class_block + e_step) * NA + a_low + a_step) * NW + w_low + w_step
                values = jnp.take(lut_table, flat_index.reshape(-1).astype(jnp.int32), axis=1)
                values = values.reshape((lut_table.shape[0],) + aero_pos.shape)
                coefficient = coefficient + (elev_weight * joint_weight)[None] * values
    coefficient = coefficient.reshape((BANDS, 3) + aero_pos.shape)
    radiance = jnp.transpose(toa_block.astype(jnp.float32), (1, 0, 2))
    scaled = coefficient[:, 0] * radiance - coefficient[:, 1]
    surface = scaled / (1.0 + coefficient[:, 2] * scaled)
    return jnp.transpose(surface, (1, 0, 2)).astype(jnp.bfloat16)


def reference(toa_bands, dark_mask, vapour, elev_class, elev_frac, kernel, lut_gain, lut_path, lut_albedo, routes, starts):
    darkness = dark_mask.astype(jnp.float32)
    blue_band = toa_bands[:, 0, :].astype(jnp.float32)
    red_band = toa_bands[:, 2, :].astype(jnp.float32)
    fields = jnp.stack([darkness * 8.0 * (blue_band - 0.5 * red_band), darkness])
    smoothed = smooth_axis(smooth_axis(fields, kernel, 1), kernel, 2)
    aerosol = smoothed[0] / jnp.maximum(smoothed[1], 1.0)
    aero_pos = (NA - 1) * jax.nn.sigmoid(aerosol)
    lut_table = jnp.stack([lut_gain, lut_path, lut_albedo], axis=1).astype(jnp.float32).reshape(BANDS * 3, NE * NA * NW)
    block_count = NR // ROW_DEV
    inputs = (toa_bands.reshape(block_count, ROW_DEV, BANDS, NC),
              aero_pos.reshape(block_count, ROW_DEV, NC),
              vapour.reshape(block_count, ROW_DEV, NC),
              elev_class.reshape(block_count, ROW_DEV, NC),
              elev_frac.reshape(block_count, ROW_DEV, NC))
    corrected = lax.map(lambda item: correct_block(item, lut_table), inputs).reshape(NR, BANDS, NC)
    segment_rows = corrected.reshape(NSEGS * SEG, BANDS * NC).astype(jnp.float32)
    summed = jnp.zeros((TILES * TILE_ROWS, BANDS * NC), dtype=jnp.float32)
    counts = jnp.zeros((TILES * TILE_ROWS,), dtype=jnp.float32)
    for route_slot in range(2):
        target = routes[:, route_slot][:, None] * TILE_ROWS + starts[:, route_slot][:, None] + jnp.arange(SEG, dtype=jnp.int32)[None, :]
        target = target.reshape(-1).astype(jnp.int32)
        summed = summed.at[target].add(segment_rows)
        counts = counts.at[target].add(jnp.ones((NSEGS * SEG,), dtype=jnp.float32))
    tile_out = (summed / jnp.maximum(counts, 1.0)[:, None]).astype(jnp.bfloat16)
    return tile_out.reshape(TILES, TILE_ROWS, BANDS, NC)
```

```python
import functools
import math

import jax
import jax.numpy as jnp
from jax import lax
from jax.experimental import pallas as pl
from jax.experimental.pallas import tpu as pltpu
from jax.sharding import PartitionSpec as P

SEG = 16
REACH = 2
CAP = 2
LANES = 128
MESH_ID = pl.DeviceIdType.MESH
SIDES = [side - REACH for side in range(REACH)] + [side + 1 for side in range(REACH)]
DIRECTIONS = [(da, dc) for da in (-1, 0, 1) for dc in (-1, 0, 1) if (da, dc) != (0, 0)]
f32 = jnp.float32
bf16 = jnp.bfloat16


def split(value):
    high = value.astype(bf16)
    return high, (value - high.astype(f32)).astype(bf16)


def toeplitz(taps, row_count, width, first):
    line = jnp.broadcast_to(taps, (8, taps.shape[1]))
    if width > taps.shape[1]:
        line = jnp.concatenate([line, jnp.zeros((8, width - taps.shape[1]), f32)], axis=1)
    stair = pltpu.roll(line, 0, 1, stride=1, stride_axis=0)
    return jnp.concatenate(
        [pltpu.roll(stair, first + 8 * group, 1) for group in range(row_count // 8)], axis=0
    )


def dot_nt(left, right):
    return lax.dot_general(left, right, (((1,), (1,)), ((), ())), preferred_element_type=f32)


def exists(position, count):
    return (position >= 0) & (position < count)


def both(position_a, count_a, position_c, count_c):
    return exists(position_a, count_a) & exists(position_c, count_c)


def smooth_kernel(
    n_along, n_across, half, levels_a, fields_ref, taps_ref, pos_ref, padded, send_sem, recv_sem
):
    along, across = lax.axis_index("along"), lax.axis_index("across")
    rows, cols = fields_ref.shape[1], fields_ref.shape[2]
    halo = (padded.shape[1] - rows) // 2
    spans = {
        -1: (slice(0, halo), slice(halo + rows, 2 * halo + rows)),
        0: (slice(0, rows), slice(halo, halo + rows)),
        1: (slice(rows - halo, rows), slice(0, halo)),
    }
    lanes = {
        -1: (slice(0, LANES), slice(LANES + cols, 2 * LANES + cols)),
        0: (slice(0, cols), slice(LANES, LANES + cols)),
        1: (slice(cols - LANES, cols), slice(0, LANES)),
    }
    barrier = pltpu.get_barrier_semaphore()
    for da, dc in DIRECTIONS:

        @pl.when(both(along + da, n_along, across + dc, n_across))
        def _():
            pl.semaphore_signal(
                barrier,
                inc=1,
                device_id={"along": along + da, "across": across + dc},
                device_id_type=MESH_ID,
            )

    def describe(number, da, dc):
        return pltpu.make_async_remote_copy(
            src_ref=fields_ref.at[:, spans[da][0], lanes[dc][0]],
            dst_ref=padded.at[:, spans[da][1], lanes[dc][1]],
            send_sem=send_sem.at[number],
            recv_sem=recv_sem.at[number],
            device_id={"along": along + da, "across": across + dc},
            device_id_type=MESH_ID,
        )

    pl.semaphore_wait(
        barrier,
        sum(
            both(along + da, n_along, across + dc, n_across).astype(jnp.int32)
            for da, dc in DIRECTIONS
        ),
    )

    for number, (da, dc) in enumerate(DIRECTIONS):

        @pl.when(both(along + da, n_along, across + dc, n_across))
        def _():
            describe(number, da, dc).start()

    padded[:, spans[0][1], lanes[0][1]] = fields_ref[...]
    for da, dc in DIRECTIONS:

        @pl.when(jnp.logical_not(both(along - da, n_along, across - dc, n_across)))
        def _():
            target = padded.at[:, spans[da][1], lanes[dc][1]]
            target[...] = jnp.zeros(target.shape, bf16)

    down_high, down_low = split(toeplitz(taps_ref[...], rows, 2 * halo + rows, halo - half))
    block = math.gcd(cols, 256)
    across_high, across_low = split(
        toeplitz(taps_ref[...], block, block + 2 * LANES, LANES - half)
    )
    for number, (da, dc) in enumerate(DIRECTIONS):

        @pl.when(both(along - da, n_along, across - dc, n_across))
        def _():
            describe(number, da, dc).wait_recv()

    down = jnp.concatenate([down_high, down_low], axis=0)
    tall = []
    for field in range(2):
        product = jnp.dot(down, padded[field], preferred_element_type=f32)
        tall.append(product[:rows] + product[rows:])
    tall_high, tall_low = split(jnp.concatenate(tall, axis=0))
    for number in range(cols // block):
        window = slice(number * block, number * block + block + 2 * LANES)
        smoothed = dot_nt(tall_high[:, window], across_high)
        smoothed += dot_nt(tall_low[:, window], across_high)
        smoothed += dot_nt(tall_high[:, window], across_low)
        aerosol = smoothed[:rows] / jnp.maximum(smoothed[rows:], 1.0)
        pos_ref[:, number * block : (number + 1) * block] = (levels_a - 1) * jax.nn.sigmoid(
            aerosol
        )
    for number, (da, dc) in enumerate(DIRECTIONS):

        @pl.when(both(along + da, n_along, across + dc, n_across))
        def _():
            describe(number, da, dc).wait_send()


def correct_kernel(
    levels,
    bands,
    routes_ref,
    starts_ref,
    toa_ref,
    pos_ref,
    vapour_ref,
    class_ref,
    frac_ref,
    lut_ref,
    corrected_ref,
    slots_ref,
    tags_ref,
    weights,
    heights,
):
    levels_e, levels_a, levels_w = levels
    seg = pl.program_id(0)
    seg_dev = routes_ref.shape[0]
    own = lax.axis_index("along")
    cols = pos_ref.shape[1]
    seg_rows = SEG * bands

    @pl.when(seg == 0)
    def _():
        slots_ref[...] = jnp.zeros(slots_ref.shape, bf16)
        lane = lax.broadcasted_iota(jnp.int32, (8, CAP * seg_rows), 1)
        for number, side in enumerate(SIDES):
            target = jnp.full((8, CAP * seg_rows), -1, jnp.int32)
            rank = jnp.int32(0)
            for s in range(seg_dev):
                hit = routes_ref[s, 1] - own == side
                place = jnp.where(hit, rank, -1)
                inside = (lane >= place * seg_rows) & (lane < (place + 1) * seg_rows) & (place >= 0)
                target = jnp.where(
                    inside, starts_ref[s, 1] * bands + lane - place * seg_rows, target
                )
                rank = rank + jnp.where(hit, 1, 0)
            tags_ref[number] = target.astype(f32)

    distance = routes_ref[seg, 1] - own
    rank = jnp.int32(0)
    for s in range(seg_dev):
        same = (routes_ref[s, 1] - own == distance) & (s < seg)
        rank = rank + jnp.where(same, 1, 0)
    side_number = jnp.where(distance < 0, distance + REACH, distance + REACH - 1)
    slot = side_number * CAP + rank

    for w in range(levels_w):
        weights[w] = jnp.maximum(0.0, 1.0 - jnp.abs(vapour_ref[...] - float(w)))
    heights[...] = class_ref[...].astype(f32) + frac_ref[...]
    node_a = lax.broadcasted_iota(jnp.int32, (levels_a, cols), 0).astype(f32)
    sub = lax.broadcasted_iota(jnp.int32, (8, cols), 0)
    lower = sub < bands
    pair_e = (sub // bands).astype(f32)
    per_tile = 8 // bands
    lut = lut_ref[...]
    quad = 16 // bands
    table_rows = levels_e * bands
    for first in range(0, SEG, quad):
        partial = []
        for row in range(first, first + quad):
            weight_a = jnp.maximum(0.0, 1.0 - jnp.abs(pos_ref[row : row + 1, :] - node_a)).astype(
                bf16
            )
            joint = jnp.concatenate(
                [
                    weight_a
                    * jnp.broadcast_to(weights[w, row : row + 1, :], (levels_a, cols)).astype(bf16)
                    for w in range(levels_w)
                ],
                axis=0,
            )
            nodes = jnp.dot(lut, joint, preferred_element_type=f32)
            height = heights[row : row + 1, :]
            sums = [None] * 3
            for k in range(table_rows // 8):
                weight_e = jnp.maximum(0.0, 1.0 - jnp.abs(height - (pair_e + float(per_tile * k))))
                for t in range(3):
                    at = t * table_rows + k * 8
                    term = nodes[at : at + 8] * weight_e
                    sums[t] = term if sums[t] is None else sums[t] + term
            partial.append(sums)
        radiance = toa_ref[first * bands : (first + quad) * bands, :].astype(f32)
        surfaces = []
        for half in range(quad // 2):
            coefficient = []
            for t in range(3):
                one, two = partial[2 * half][t], partial[2 * half + 1][t]
                kept = jnp.where(lower, one, two)
                moved = pltpu.roll(jnp.where(lower, two, one), bands, 0)
                coefficient.append(kept + moved)
            scaled = coefficient[0] * radiance[half * 8 : half * 8 + 8] - coefficient[1]
            surfaces.append(scaled / (1.0 + coefficient[2] * scaled))
        surface = jnp.concatenate(surfaces, axis=0).astype(bf16)
        corrected_ref[seg, first * bands : (first + quad) * bands, :] = surface
        slots_ref[slot, first * bands : (first + quad) * bands, :] = surface


def place_kernel(
    n_along,
    bands,
    routes_ref,
    starts_ref,
    corrected_ref,
    slots_ref,
    tags_ref,
    out_ref,
    got_rows,
    got_tags,
    send_sem,
    recv_sem,
):
    along = lax.axis_index("along")
    barrier = pltpu.get_barrier_semaphore()
    seg_dev, seg_rows = corrected_ref.shape[0], corrected_ref.shape[1]
    cols = corrected_ref.shape[2]
    out_rows = out_ref.shape[0]
    for side in SIDES:

        @pl.when(exists(along + side, n_along))
        def _():
            pl.semaphore_signal(
                barrier, inc=1, device_id={"along": along + side}, device_id_type=MESH_ID
            )

    pl.semaphore_wait(
        barrier, sum(exists(along + side, n_along).astype(jnp.int32) for side in SIDES)
    )

    def describe(number):
        side = SIDES[number]
        rows = pltpu.make_async_remote_copy(
            src_ref=slots_ref.at[pl.ds(number * CAP, CAP)],
            dst_ref=got_rows.at[number],
            send_sem=send_sem.at[number],
            recv_sem=recv_sem.at[number],
            device_id={"along": along + side},
            device_id_type=MESH_ID,
        )
        tags = pltpu.make_async_remote_copy(
            src_ref=tags_ref.at[number],
            dst_ref=got_tags.at[number],
            send_sem=send_sem.at[len(SIDES) + number],
            recv_sem=recv_sem.at[len(SIDES) + number],
            device_id={"along": along + side},
            device_id_type=MESH_ID,
        )
        return tags, rows

    order = sorted(range(len(SIDES)), key=lambda number: abs(SIDES[number]))
    for number in order:

        @pl.when(exists(along + SIDES[number], n_along))
        def _():
            for copy in describe(number):
                copy.start()

        @pl.when(jnp.logical_not(exists(along - SIDES[number], n_along)))
        def _():
            got_rows[number] = jnp.zeros(got_rows.shape[1:], bf16)
            got_tags[number] = jnp.full(got_tags.shape[1:], -1.0, f32)

    def placed(target):
        row = lax.broadcasted_iota(jnp.int32, (out_rows, target.shape[1]), 0).astype(f32)
        return jnp.where(row == target, 1.0, 0.0)

    lane = lax.broadcasted_iota(jnp.int32, (1, seg_dev * seg_rows), 1)
    target = jnp.full((1, seg_dev * seg_rows), -1, jnp.int32)
    for s in range(seg_dev):
        inside = (lane >= s * seg_rows) & (lane < (s + 1) * seg_rows)
        inside = inside & (routes_ref[s, 0] == along)
        target = jnp.where(inside, starts_ref[s, 0] * bands + lane - s * seg_rows, target)
    matrix = placed(target.astype(f32))
    count = jnp.sum(matrix, axis=1, keepdims=True)
    summed = jnp.dot(
        matrix.astype(bf16),
        corrected_ref[...].reshape(seg_dev * seg_rows, cols),
        preferred_element_type=f32,
    )
    for number in order:

        @pl.when(exists(along - SIDES[number], n_along))
        def _():
            for copy in describe(number):
                copy.wait_recv()

        matrix = placed(got_tags[number, 0:1, :])
        count = count + jnp.sum(matrix, axis=1, keepdims=True)
        summed = summed + jnp.dot(
            matrix.astype(bf16),
            got_rows[number].reshape(CAP * seg_rows, cols),
            preferred_element_type=f32,
        )
    out_ref[...] = (summed / jnp.maximum(count, 1.0)).astype(bf16)
    for number in order:

        @pl.when(exists(along + SIDES[number], n_along))
        def _():
            for copy in describe(number):
                copy.wait_send()


def body(
    n_along,
    n_across,
    toa_bands,
    dark_mask,
    vapour,
    elev_class,
    elev_frac,
    kernel,
    lut_gain,
    lut_path,
    lut_albedo,
    routes,
    starts,
):
    rows, bands, cols = toa_bands.shape
    half = kernel.shape[0] // 2
    halo = -(-half // 16) * 16
    levels = lut_gain.shape[1:]
    levels_e, levels_a, levels_w = levels
    seg_dev = routes.shape[0]
    seg_rows = SEG * bands
    side_count = len(SIDES)
    vmem = pl.BlockSpec(memory_space=pltpu.VMEM)
    smem = pl.BlockSpec(memory_space=pltpu.SMEM)

    darkness = dark_mask.astype(f32)
    weighted = darkness * 8.0 * (toa_bands[:, 0, :].astype(f32) - 0.5 * toa_bands[:, 2, :].astype(f32))
    fields = jnp.stack([weighted, darkness]).astype(bf16)
    taps = jnp.pad(kernel, (0, LANES - kernel.shape[0]))[None]
    lut = (
        jnp.stack([lut_gain, lut_path, lut_albedo])
        .transpose(0, 2, 1, 4, 3)
        .reshape(3 * levels_e * bands, levels_w * levels_a)
    )
    flat = toa_bands.reshape(rows * bands, cols)

    aero_pos = pl.pallas_call(
        functools.partial(smooth_kernel, n_along, n_across, half, levels_a),
        out_shape=jax.ShapeDtypeStruct((rows, cols), f32),
        in_specs=[vmem, vmem],
        out_specs=vmem,
        scratch_shapes=[
            pltpu.VMEM((2, rows + 2 * halo, cols + 2 * LANES), bf16),
            pltpu.SemaphoreType.DMA((len(DIRECTIONS),)),
            pltpu.SemaphoreType.DMA((len(DIRECTIONS),)),
        ],
        compiler_params=pltpu.CompilerParams(collective_id=0, has_side_effects=True),
        name="smooth",
    )(fields, taps)

    def rows_spec(count):
        return pl.BlockSpec((count, cols), lambda s: (s, 0))

    corrected, slots, tags = pl.pallas_call(
        functools.partial(correct_kernel, levels, bands),
        grid=(seg_dev,),
        out_shape=(
            jax.ShapeDtypeStruct((seg_dev, seg_rows, cols), bf16),
            jax.ShapeDtypeStruct((side_count * CAP, seg_rows, cols), bf16),
            jax.ShapeDtypeStruct((side_count, 8, CAP * seg_rows), f32),
        ),
        in_specs=[
            smem,
            smem,
            rows_spec(seg_rows),
            rows_spec(SEG),
            rows_spec(SEG),
            rows_spec(SEG),
            rows_spec(SEG),
            vmem,
        ],
        out_specs=(vmem, vmem, vmem),
        scratch_shapes=[
            pltpu.VMEM((levels_w, SEG, cols), f32),
            pltpu.VMEM((SEG, cols), f32),
        ],
        compiler_params=pltpu.CompilerParams(dimension_semantics=("arbitrary",)),
        name="correct",
    )(routes, starts, flat, aero_pos, vapour, elev_class, elev_frac, lut)

    out = pl.pallas_call(
        functools.partial(place_kernel, n_along, bands),
        out_shape=jax.ShapeDtypeStruct((rows * bands, cols), bf16),
        in_specs=[smem, smem, vmem, vmem, vmem],
        out_specs=vmem,
        scratch_shapes=[
            pltpu.VMEM((side_count, CAP, seg_rows, cols), bf16),
            pltpu.VMEM((side_count, 8, CAP * seg_rows), f32),
            pltpu.SemaphoreType.DMA((2 * side_count,)),
            pltpu.SemaphoreType.DMA((2 * side_count,)),
        ],
        compiler_params=pltpu.CompilerParams(collective_id=1, has_side_effects=True),
        name="place",
    )(routes, starts, corrected, slots, tags)
    return out.reshape(1, rows, bands, cols)


def solution(mesh):
    in_specs = (
        P(("groups", "along"), None, "across"),
        P(("groups", "along"), "across"),
        P(("groups", "along"), "across"),
        P(("groups", "along"), "across"),
        P(("groups", "along"), "across"),
        P(),
        P(),
        P(),
        P(),
        P(("groups", "along"), None),
        P(("groups", "along"), None),
    )
    out_specs = P(("groups", "along"), None, None, "across")
    run = functools.partial(body, mesh.shape["along"], mesh.shape["across"])
    return jax.shard_map(run, mesh=mesh, in_specs=in_specs, out_specs=out_specs, check_vma=False)
```

```python
import functools
import math

import jax
import jax.numpy as jnp
from jax import lax
from jax.experimental import pallas as pl
from jax.experimental.pallas import tpu as pltpu
from jax.sharding import PartitionSpec as P

SEG = 16
REACH = 2
CAP = 2
LANES = 128
MESH_ID = pl.DeviceIdType.MESH
SIDES = [side - REACH for side in range(REACH)] + [side + 1 for side in range(REACH)]
DIRECTIONS = [(da, dc) for da in (-1, 0, 1) for dc in (-1, 0, 1) if (da, dc) != (0, 0)]
f32 = jnp.float32
bf16 = jnp.bfloat16


def split(value):
    high = value.astype(bf16)
    return high, (value - high.astype(f32)).astype(bf16)


def toeplitz(taps, row_count, width, first):
    line = jnp.broadcast_to(taps, (8, taps.shape[1]))
    if width > taps.shape[1]:
        line = jnp.concatenate([line, jnp.zeros((8, width - taps.shape[1]), f32)], axis=1)
    stair = pltpu.roll(line, 0, 1, stride=1, stride_axis=0)
    return jnp.concatenate(
        [pltpu.roll(stair, first + 8 * group, 1) for group in range(row_count // 8)], axis=0
    )


def dot_nt(left, right):
    return lax.dot_general(left, right, (((1,), (1,)), ((), ())), preferred_element_type=f32)


def exists(position, count):
    return (position >= 0) & (position < count)


def both(position_a, count_a, position_c, count_c):
    return exists(position_a, count_a) & exists(position_c, count_c)


def prep_kernel(toa_ref, mask_ref, routes_ref, starts_ref, flat_ref, fields_ref, tags_ref):
    rows, bands, cols = toa_ref.shape
    own = lax.axis_index("along")
    flat = toa_ref[...].astype(f32).reshape(rows * bands, cols).astype(bf16)
    flat_ref[...] = flat
    row = lax.broadcasted_iota(jnp.int32, (rows, rows * bands), 0) * bands
    col = lax.broadcasted_iota(jnp.int32, (rows, rows * bands), 1)
    pick = jnp.where(col == row, 8.0, 0.0) + jnp.where(col == row + 2, -4.0, 0.0)
    darkness = mask_ref[...].astype(f32)
    value = jnp.dot(pick.astype(bf16), flat, preferred_element_type=f32)
    fields_ref[0] = (darkness * value).astype(bf16)
    fields_ref[1] = darkness.astype(bf16)
    seg_rows = SEG * bands
    lane = lax.broadcasted_iota(jnp.int32, (8, CAP * seg_rows), 1)
    for number, side in enumerate(SIDES):
        target = jnp.full((8, CAP * seg_rows), -1, jnp.int32)
        rank = jnp.int32(0)
        for s in range(routes_ref.shape[1]):
            hit = routes_ref[1, s] - own == side
            place = jnp.where(hit, rank, -1)
            inside = (lane >= place * seg_rows) & (lane < (place + 1) * seg_rows) & (place >= 0)
            target = jnp.where(inside, starts_ref[1, s] * bands + lane - place * seg_rows, target)
            rank = rank + jnp.where(hit, 1, 0)
        tags_ref[number] = target.astype(f32)


def main_kernel(
    n_along,
    n_across,
    bands,
    levels,
    routes_ref,
    starts_ref,
    fields_ref,
    tags_ref,
    taps_ref,
    gain_ref,
    path_ref,
    albedo_ref,
    toa_hbm,
    vapour_hbm,
    class_hbm,
    frac_hbm,
    out_ref,
    toa_ref,
    vapour_ref,
    class_ref,
    frac_ref,
    taps_pad,
    padded,
    pos_ref,
    weights,
    heights,
    corrected,
    slots,
    got_rows,
    got_tags,
    load_sem,
    halo_send,
    halo_recv,
    tag_send,
    tag_recv,
    slot_send,
    slot_recv,
):
    along, across = lax.axis_index("along"), lax.axis_index("across")
    levels_e, levels_a, levels_w = levels
    rows, cols = fields_ref.shape[1], fields_ref.shape[2]
    halo = (padded.shape[1] - rows) // 2
    half = taps_ref.shape[1] // 2
    chunks, seg_dev, seg_rows, width = corrected.shape
    loads = [
        pltpu.make_async_copy(source, target, load_sem.at[number])
        for number, (source, target) in enumerate(
            (
                (vapour_hbm, vapour_ref),
                (class_hbm, class_ref),
                (frac_hbm, frac_ref),
                (toa_hbm, toa_ref),
            )
        )
    ]
    barrier = pltpu.get_barrier_semaphore()
    peers = DIRECTIONS + [(side, 0) for side in SIDES if (side, 0) not in DIRECTIONS]
    for da, dc in peers:

        @pl.when(both(along + da, n_along, across + dc, n_across))
        def _():
            pl.semaphore_signal(
                barrier,
                inc=1,
                device_id={"along": along + da, "across": across + dc},
                device_id_type=MESH_ID,
            )

    for load in loads:
        load.start()
    spans = {
        -1: (slice(0, halo), slice(halo + rows, 2 * halo + rows)),
        0: (slice(0, rows), slice(halo, halo + rows)),
        1: (slice(rows - halo, rows), slice(0, halo)),
    }
    lanes = {
        -1: (slice(0, LANES), slice(LANES + cols, 2 * LANES + cols)),
        0: (slice(0, cols), slice(LANES, LANES + cols)),
        1: (slice(cols - LANES, cols), slice(0, LANES)),
    }

    def halo_copy(number, da, dc):
        return pltpu.make_async_remote_copy(
            src_ref=fields_ref.at[:, spans[da][0], lanes[dc][0]],
            dst_ref=padded.at[:, spans[da][1], lanes[dc][1]],
            send_sem=halo_send.at[number],
            recv_sem=halo_recv.at[number],
            device_id={"along": along + da, "across": across + dc},
            device_id_type=MESH_ID,
        )

    def tag_copy(number):
        return pltpu.make_async_remote_copy(
            src_ref=tags_ref.at[number],
            dst_ref=got_tags.at[number],
            send_sem=tag_send.at[number],
            recv_sem=tag_recv.at[number],
            device_id={"along": along + SIDES[number]},
            device_id_type=MESH_ID,
        )

    def slot_copy(chunk, number):
        return pltpu.make_async_remote_copy(
            src_ref=slots.at[chunk, pl.ds(number * CAP, CAP)],
            dst_ref=got_rows.at[chunk, number],
            send_sem=slot_send.at[chunk, number],
            recv_sem=slot_recv.at[chunk, number],
            device_id={"along": along + SIDES[number]},
            device_id_type=MESH_ID,
        )

    pl.semaphore_wait(
        barrier,
        sum(
            both(along + da, n_along, across + dc, n_across).astype(jnp.int32) for da, dc in peers
        ),
    )
    for number, (da, dc) in enumerate(DIRECTIONS):

        @pl.when(both(along + da, n_along, across + dc, n_across))
        def _():
            halo_copy(number, da, dc).start()

    order = sorted(range(len(SIDES)), key=lambda number: abs(SIDES[number]))
    for number in order:

        @pl.when(exists(along + SIDES[number], n_along))
        def _():
            tag_copy(number).start()

        @pl.when(jnp.logical_not(exists(along - SIDES[number], n_along)))
        def _():
            got_rows[:, number] = jnp.zeros((chunks, CAP, seg_rows, width), bf16)
            got_tags[number] = jnp.full(got_tags.shape[1:], -1.0, f32)

    padded[:, spans[0][1], lanes[0][1]] = fields_ref[...]
    for da, dc in DIRECTIONS:

        @pl.when(jnp.logical_not(both(along - da, n_along, across - dc, n_across)))
        def _():
            target = padded.at[:, spans[da][1], lanes[dc][1]]
            target[...] = jnp.zeros(target.shape, bf16)

    taps_pad[...] = jnp.zeros(taps_pad.shape, f32)
    taps_pad[0:1, 0 : taps_ref.shape[1]] = taps_ref[...]
    taps = taps_pad[0:1, :]
    down_high, down_low = split(toeplitz(taps, rows, 2 * halo + rows, halo - half))
    down = jnp.concatenate([down_high, down_low], axis=0)
    block = width
    across_high, across_low = split(toeplitz(taps, block, block + 2 * LANES, LANES - half))

    node_count = levels_w * levels_a
    tables = jnp.concatenate([gain_ref[...], path_ref[...], albedo_ref[...]], axis=0)
    spread_a = lax.broadcasted_iota(jnp.int32, (levels_a, node_count), 0)
    spread_n = lax.broadcasted_iota(jnp.int32, (levels_a, node_count), 1)
    spread = jnp.where(spread_n % levels_a == spread_a, 1.0, 0.0).astype(bf16)
    wide = jnp.dot(tables, spread, preferred_element_type=f32)
    wide_w = lax.broadcasted_iota(jnp.int32, wide.shape, 0) % levels_w
    wide_n = lax.broadcasted_iota(jnp.int32, wide.shape, 1) // levels_a
    wide = jnp.where(wide_w == wide_n, wide, 0.0).astype(bf16)
    table_rows = levels_e * bands
    into = lax.broadcasted_iota(jnp.int32, (3 * table_rows, wide.shape[0]), 0)
    source = lax.broadcasted_iota(jnp.int32, (3 * table_rows, wide.shape[0]), 1) // levels_w
    within = into % table_rows
    wanted = into - within + (within % bands) * levels_e + within // bands
    lut = jnp.dot(
        jnp.where(source == wanted, 1.0, 0.0).astype(bf16), wide, preferred_element_type=f32
    ).astype(bf16)

    for load in loads:
        load.wait()
    for w in range(levels_w):
        weights[w] = jnp.maximum(0.0, 1.0 - jnp.abs(vapour_ref[...] - float(w)))
    heights[...] = class_ref[...].astype(f32) + frac_ref[...]

    for number, (da, dc) in enumerate(DIRECTIONS):

        @pl.when(both(along - da, n_along, across - dc, n_across))
        def _():
            halo_copy(number, da, dc).wait_recv()

    tall = []
    for field in range(2):
        product = jnp.dot(down, padded[field], preferred_element_type=f32)
        tall.append(product[:rows] + product[rows:])
    tall_high, tall_low = split(jnp.concatenate(tall, axis=0))
    for number in range(chunks):
        window = slice(number * block, number * block + block + 2 * LANES)
        smoothed = dot_nt(tall_high[:, window], across_high)
        smoothed += dot_nt(tall_low[:, window], across_high)
        smoothed += dot_nt(tall_high[:, window], across_low)
        aerosol = smoothed[:rows] / jnp.maximum(smoothed[rows:], 1.0)
        pos_ref[:, number * block : (number + 1) * block] = (levels_a - 1) * jax.nn.sigmoid(
            aerosol
        )

    chosen = []
    for number, side in enumerate(SIDES):
        rank = jnp.int32(0)
        first = [jnp.int32(0) for _ in range(CAP)]
        for s in range(seg_dev):
            hit = routes_ref[1, s] - along == side
            for k in range(CAP):
                first[k] = jnp.where(hit & (rank == k), s, first[k])
            rank = rank + jnp.where(hit, 1, 0)
        chosen.append(first)

    node_a = lax.broadcasted_iota(jnp.int32, (levels_a, width), 0).astype(f32)
    sub = lax.broadcasted_iota(jnp.int32, (8, width), 0)
    lower = sub < bands
    pair_e = (sub // bands).astype(f32)
    per_tile = 8 // bands
    quad = 16 // bands

    def correct(chunk, seg):
        at_cols = slice(chunk * width, (chunk + 1) * width)
        base = pl.multiple_of(seg * SEG, SEG)
        base_flat = pl.multiple_of(seg * seg_rows, seg_rows)
        position = pos_ref[pl.ds(base, SEG), at_cols]
        height_rows = heights[pl.ds(base, SEG), at_cols]
        for first in range(0, SEG, quad):
            partial = []
            for row in range(first, first + quad):
                weight_a = jnp.maximum(0.0, 1.0 - jnp.abs(position[row : row + 1] - node_a))
                joint = jnp.concatenate(
                    [
                        (weight_a * weights[w, pl.ds(base + row, 1), at_cols]).astype(bf16)
                        for w in range(levels_w)
                    ],
                    axis=0,
                )
                nodes = jnp.dot(lut, joint, preferred_element_type=f32)
                height = height_rows[row : row + 1]
                sums = [None] * 3
                for k in range(table_rows // 8):
                    weight_e = jnp.maximum(
                        0.0, 1.0 - jnp.abs(height - (pair_e + float(per_tile * k)))
                    )
                    for t in range(3):
                        at = t * table_rows + k * 8
                        term = nodes[at : at + 8] * weight_e
                        sums[t] = term if sums[t] is None else sums[t] + term
                partial.append(sums)
            radiance = toa_ref[pl.ds(base_flat + first * bands, quad * bands), at_cols].astype(f32)
            surfaces = []
            for part in range(quad // 2):
                coefficient = []
                for t in range(3):
                    one, two = partial[2 * part][t], partial[2 * part + 1][t]
                    kept = jnp.where(lower, one, two)
                    moved = pltpu.roll(jnp.where(lower, two, one), bands, 0)
                    coefficient.append(kept + moved)
                scaled = coefficient[0] * radiance[part * 8 : part * 8 + 8] - coefficient[1]
                surfaces.append(scaled / (1.0 + coefficient[2] * scaled))
            corrected[chunk, seg, first * bands : (first + quad) * bands, :] = jnp.concatenate(
                surfaces, axis=0
            ).astype(bf16)

    def correct_from(chunk, low, high):
        def step(seg, carry):
            correct(chunk, seg)
            return carry

        lax.fori_loop(low, high, step, 0)

    def start_slots(chunk):
        for number in order:

            @pl.when(exists(along + SIDES[number], n_along))
            def _():
                slot_copy(chunk, number).start()

    def placed(target):
        row = lax.broadcasted_iota(jnp.int32, (rows * bands, target.shape[1]), 0).astype(f32)
        return jnp.where(row == target, 1.0, 0.0)

    for chunk in range(chunks):
        correct_from(chunk, 0, 1)
        if chunk:
            start_slots(chunk - 1)
        correct_from(chunk, 1, seg_dev)
        for number in range(len(SIDES)):
            for k in range(CAP):
                slots[chunk, number * CAP + k] = corrected[chunk, chosen[number][k]]

    lane = lax.broadcasted_iota(jnp.int32, (1, seg_dev * seg_rows), 1)
    target = jnp.full((1, seg_dev * seg_rows), -1, jnp.int32)
    for s in range(seg_dev):
        inside = (lane >= s * seg_rows) & (lane < (s + 1) * seg_rows)
        inside = inside & (routes_ref[0, s] == along)
        target = jnp.where(inside, starts_ref[0, s] * bands + lane - s * seg_rows, target)
    own = placed(target.astype(f32))
    start_slots(chunks - 1)
    count = jnp.sum(own, axis=1, keepdims=True)
    own = own.astype(bf16)
    matrices = {}
    for number in order:

        @pl.when(exists(along - SIDES[number], n_along))
        def _():
            tag_copy(number).wait_recv()

        matrix = placed(got_tags[number, 0:1, :])
        count = count + jnp.sum(matrix, axis=1, keepdims=True)
        matrices[number] = matrix.astype(bf16)
    count = jnp.maximum(count, 1.0)
    for chunk in range(chunks):
        summed = jnp.dot(
            own, corrected[chunk].reshape(seg_dev * seg_rows, width), preferred_element_type=f32
        )
        for number in order:

            @pl.when(exists(along - SIDES[number], n_along))
            def _():
                slot_copy(chunk, number).wait_recv()

            summed = summed + jnp.dot(
                matrices[number],
                got_rows[chunk, number].reshape(CAP * seg_rows, width),
                preferred_element_type=f32,
            )
        result = (summed / count).reshape(rows, bands, width)
        out_ref[:, :, chunk * width : (chunk + 1) * width] = result.astype(bf16)
    for number, (da, dc) in enumerate(DIRECTIONS):

        @pl.when(both(along + da, n_along, across + dc, n_across))
        def _():
            halo_copy(number, da, dc).wait_send()

    for number in order:

        @pl.when(exists(along + SIDES[number], n_along))
        def _():
            tag_copy(number).wait_send()
            for chunk in range(chunks):
                slot_copy(chunk, number).wait_send()


def body(
    n_along,
    n_across,
    toa_bands,
    dark_mask,
    vapour,
    elev_class,
    elev_frac,
    kernel,
    lut_gain,
    lut_path,
    lut_albedo,
    routes,
    starts,
):
    rows, bands, cols = toa_bands.shape
    half = kernel.shape[0] // 2
    halo = -(-half // 16) * 16
    levels = lut_gain.shape[1:]
    levels_e, levels_a, levels_w = levels
    seg_dev = routes.shape[0]
    seg_rows = SEG * bands
    side_count = len(SIDES)
    width = math.gcd(cols, 256)
    chunks = cols // width
    vmem = pl.BlockSpec(memory_space=pltpu.VMEM)
    smem = pl.BlockSpec(memory_space=pltpu.SMEM)
    anywhere = pl.BlockSpec(memory_space=pl.ANY)
    dma = pltpu.SemaphoreType.DMA

    def table(lut):
        return lut.transpose(0, 1, 3, 2).reshape(bands * levels_e * levels_w, levels_a)

    flat, fields, tags = pl.pallas_call(
        prep_kernel,
        out_shape=(
            jax.ShapeDtypeStruct((rows * bands, cols), bf16),
            jax.ShapeDtypeStruct((2, rows, cols), bf16),
            jax.ShapeDtypeStruct((side_count, 8, CAP * seg_rows), f32),
        ),
        in_specs=[vmem, vmem, smem, smem],
        out_specs=(vmem, vmem, vmem),
        name="prep",
    )(toa_bands, dark_mask, routes.T, starts.T)

    out = pl.pallas_call(
        functools.partial(main_kernel, n_along, n_across, bands, levels),
        out_shape=jax.ShapeDtypeStruct((rows, bands, cols), bf16),
        in_specs=[smem, smem] + [vmem] * 6 + [anywhere] * 4,
        out_specs=vmem,
        scratch_shapes=[
            pltpu.VMEM((rows * bands, cols), bf16),
            pltpu.VMEM((rows, cols), f32),
            pltpu.VMEM((rows, cols), jnp.int32),
            pltpu.VMEM((rows, cols), f32),
            pltpu.VMEM((8, LANES), f32),
            pltpu.VMEM((2, rows + 2 * halo, cols + 2 * LANES), bf16),
            pltpu.VMEM((rows, cols), f32),
            pltpu.VMEM((levels_w, rows, cols), f32),
            pltpu.VMEM((rows, cols), f32),
            pltpu.VMEM((chunks, seg_dev, seg_rows, width), bf16),
            pltpu.VMEM((chunks, side_count * CAP, seg_rows, width), bf16),
            pltpu.VMEM((chunks, side_count, CAP, seg_rows, width), bf16),
            pltpu.VMEM((side_count, 8, CAP * seg_rows), f32),
            dma((4,)),
            dma((len(DIRECTIONS),)),
            dma((len(DIRECTIONS),)),
            dma((side_count,)),
            dma((side_count,)),
            dma((chunks, side_count)),
            dma((chunks, side_count)),
        ],
        compiler_params=pltpu.CompilerParams(collective_id=0, has_side_effects=True),
        name="main",
    )(
        routes.T,
        starts.T,
        fields,
        tags,
        kernel[None],
        table(lut_gain),
        table(lut_path),
        table(lut_albedo),
        flat,
        vapour,
        elev_class,
        elev_frac,
    )
    return out[None]


def solution(mesh):
    in_specs = (
        P(("groups", "along"), None, "across"),
        P(("groups", "along"), "across"),
        P(("groups", "along"), "across"),
        P(("groups", "along"), "across"),
        P(("groups", "along"), "across"),
        P(),
        P(),
        P(),
        P(),
        P(("groups", "along"), None),
        P(("groups", "along"), None),
    )
    out_specs = P(("groups", "along"), None, None, "across")
    run = functools.partial(body, mesh.shape["along"], mesh.shape["across"])
    return jax.shard_map(run, mesh=mesh, in_specs=in_specs, out_specs=out_specs, check_vma=False)
```

```python
import functools
import math

import jax
import jax.numpy as jnp
from jax import lax
from jax.experimental import pallas as pl
from jax.experimental.pallas import tpu as pltpu
from jax.sharding import PartitionSpec as P

SEG = 16
REACH = 2
CAP = 2
LANES = 128
WIDTH = 256
MESH_ID = pl.DeviceIdType.MESH
SIDES = [side - REACH for side in range(REACH)] + [side + 1 for side in range(REACH)]
DIRECTIONS = [(da, dc) for da in (-1, 0, 1) for dc in (-1, 0, 1) if (da, dc) != (0, 0)]
f32 = jnp.float32
bf16 = jnp.bfloat16


def split(value):
    high = value.astype(bf16)
    return high, (value - high.astype(f32)).astype(bf16)


def toeplitz(taps, row_count, width, first):
    line = jnp.broadcast_to(taps, (8, taps.shape[1]))
    if width > taps.shape[1]:
        line = jnp.concatenate([line, jnp.zeros((8, width - taps.shape[1]), f32)], axis=1)
    stair = pltpu.roll(line, 0, 1, stride=1, stride_axis=0)
    return jnp.concatenate(
        [pltpu.roll(stair, first + 8 * group, 1) for group in range(row_count // 8)], axis=0
    )


def dot_nt(left, right):
    return lax.dot_general(left, right, (((1,), (1,)), ((), ())), preferred_element_type=f32)


def exists(position, count):
    return (position >= 0) & (position < count)


def both(position_a, count_a, position_c, count_c):
    return exists(position_a, count_a) & exists(position_c, count_c)


def main_kernel(
    n_along,
    n_across,
    bands,
    levels,
    routes_ref,
    starts_ref,
    toa_hbm,
    mask_hbm,
    taps_hbm,
    gain_hbm,
    path_hbm,
    albedo_hbm,
    vapour_hbm,
    class_hbm,
    frac_hbm,
    out_ref,
    raw_ref,
    mask_ref,
    taps_ref,
    gain_ref,
    path_ref,
    albedo_ref,
    vapour_ref,
    class_ref,
    frac_ref,
    toa_ref,
    fields_ref,
    tags_ref,
    taps_pad,
    padded,
    tall_high,
    tall_low,
    pos_ref,
    weights,
    heights,
    corrected,
    slots,
    got_rows,
    got_tags,
    load_sem,
    halo_send,
    halo_recv,
    tag_send,
    tag_recv,
    slot_send,
    slot_recv,
):
    along, across = lax.axis_index("along"), lax.axis_index("across")
    levels_e, levels_a, levels_w = levels
    rows, _, cols = toa_hbm.shape
    halo = (padded.shape[1] - rows) // 2
    half = taps_hbm.shape[1] // 2
    chunks, seg_dev, seg_rows, width = corrected.shape
    loads = [
        pltpu.make_async_copy(source, target, load_sem.at[number])
        for number, (source, target) in enumerate(
            (
                (toa_hbm, raw_ref),
                (mask_hbm, mask_ref),
                (taps_hbm, taps_ref),
                (gain_hbm, gain_ref),
                (path_hbm, path_ref),
                (albedo_hbm, albedo_ref),
                (vapour_hbm, vapour_ref),
                (class_hbm, class_ref),
                (frac_hbm, frac_ref),
            )
        )
    ]
    for load in loads:
        load.start()
    barrier = pltpu.get_barrier_semaphore()
    peers = DIRECTIONS + [(side, 0) for side in SIDES if (side, 0) not in DIRECTIONS]
    for da, dc in peers:

        @pl.when(both(along + da, n_along, across + dc, n_across))
        def _():
            pl.semaphore_signal(
                barrier,
                inc=1,
                device_id={"along": along + da, "across": across + dc},
                device_id_type=MESH_ID,
            )

    for load in loads[:2]:
        load.wait()
    flat = raw_ref[...].astype(f32).reshape(rows * bands, cols).astype(bf16)
    row = lax.broadcasted_iota(jnp.int32, (rows, rows * bands), 0) * bands
    col = lax.broadcasted_iota(jnp.int32, (rows, rows * bands), 1)
    pick = jnp.where(col == row, 8.0, 0.0) + jnp.where(col == row + 2, -4.0, 0.0)
    darkness = mask_ref[...].astype(f32)
    value = jnp.dot(pick.astype(bf16), flat, preferred_element_type=f32)
    fields_ref[0] = (darkness * value).astype(bf16)
    fields_ref[1] = darkness.astype(bf16)
    padded[:, halo : halo + rows, LANES : LANES + cols] = fields_ref[...]
    lane = lax.broadcasted_iota(jnp.int32, (8, CAP * seg_rows), 1)
    for number, side in enumerate(SIDES):
        target = jnp.full((8, CAP * seg_rows), -1, jnp.int32)
        rank = jnp.int32(0)
        for s in range(seg_dev):
            hit = routes_ref[1, s] - along == side
            place = jnp.where(hit, rank, -1)
            inside = (lane >= place * seg_rows) & (lane < (place + 1) * seg_rows) & (place >= 0)
            target = jnp.where(inside, starts_ref[1, s] * bands + lane - place * seg_rows, target)
            rank = rank + jnp.where(hit, 1, 0)
        tags_ref[number] = target.astype(f32)
    spans = {
        -1: (slice(0, halo), slice(halo + rows, 2 * halo + rows)),
        0: (slice(0, rows), slice(halo, halo + rows)),
        1: (slice(rows - halo, rows), slice(0, halo)),
    }
    lanes = {
        -1: (slice(0, LANES), slice(LANES + cols, 2 * LANES + cols)),
        0: (slice(0, cols), slice(LANES, LANES + cols)),
        1: (slice(cols - LANES, cols), slice(0, LANES)),
    }

    copies = []
    for da, dc in DIRECTIONS:
        if dc:
            copies.append((da, dc, lanes[dc][0], lanes[dc][1], 0 if dc > 0 else chunks - 1))
    begin = 0
    for chunk in range(chunks):
        end = min(cols, (chunk + 1) * width + LANES)
        if end > begin:
            for da in (-1, 1):
                copies.append(
                    (da, 0, slice(begin, end), slice(LANES + begin, LANES + end), chunk)
                )
        begin = end

    def halo_copy(number):
        da, dc, source, target, _ = copies[number]
        return pltpu.make_async_remote_copy(
            src_ref=fields_ref.at[:, spans[da][0], source],
            dst_ref=padded.at[:, spans[da][1], target],
            send_sem=halo_send.at[number],
            recv_sem=halo_recv.at[number],
            device_id={"along": along + da, "across": across + dc},
            device_id_type=MESH_ID,
        )

    def tag_copy(number):
        return pltpu.make_async_remote_copy(
            src_ref=tags_ref.at[number],
            dst_ref=got_tags.at[number],
            send_sem=tag_send.at[number],
            recv_sem=tag_recv.at[number],
            device_id={"along": along + SIDES[number]},
            device_id_type=MESH_ID,
        )

    def slot_copy(chunk, number):
        return pltpu.make_async_remote_copy(
            src_ref=slots.at[chunk, pl.ds(number * CAP, CAP)],
            dst_ref=got_rows.at[chunk, number],
            send_sem=slot_send.at[chunk, number],
            recv_sem=slot_recv.at[chunk, number],
            device_id={"along": along + SIDES[number]},
            device_id_type=MESH_ID,
        )

    pl.semaphore_wait(
        barrier,
        sum(
            both(along + da, n_along, across + dc, n_across).astype(jnp.int32) for da, dc in peers
        ),
    )
    for number, (da, dc, _, _, _) in enumerate(copies):

        @pl.when(both(along + da, n_along, across + dc, n_across))
        def _():
            halo_copy(number).start()

    order = sorted(range(len(SIDES)), key=lambda number: abs(SIDES[number]))
    for number in order:

        @pl.when(exists(along + SIDES[number], n_along))
        def _():
            tag_copy(number).start()

        @pl.when(jnp.logical_not(exists(along - SIDES[number], n_along)))
        def _():
            got_rows[:, number] = jnp.zeros((chunks, CAP, seg_rows, width), bf16)
            got_tags[number] = jnp.full(got_tags.shape[1:], -1.0, f32)

    toa_ref[...] = flat
    for da, dc in DIRECTIONS:

        @pl.when(jnp.logical_not(both(along - da, n_along, across - dc, n_across)))
        def _():
            target = padded.at[:, spans[da][1], lanes[dc][1]]
            target[...] = jnp.zeros(target.shape, bf16)

    for load in loads[2:6]:
        load.wait()
    taps_pad[...] = jnp.zeros(taps_pad.shape, f32)
    taps_pad[0:1, 0 : taps_ref.shape[1]] = taps_ref[...]
    taps = taps_pad[0:1, :]
    down_high, down_low = split(toeplitz(taps, rows, 2 * halo + rows, halo - half))
    down = jnp.concatenate([down_high, down_low], axis=0)
    block = width
    across_high, across_low = split(toeplitz(taps, block, block + 2 * LANES, LANES - half))

    node_count = levels_w * levels_a
    tables = jnp.concatenate([gain_ref[...], path_ref[...], albedo_ref[...]], axis=0)
    spread_a = lax.broadcasted_iota(jnp.int32, (levels_a, node_count), 0)
    spread_n = lax.broadcasted_iota(jnp.int32, (levels_a, node_count), 1)
    spread = jnp.where(spread_n % levels_a == spread_a, 1.0, 0.0).astype(bf16)
    wide = jnp.dot(tables, spread, preferred_element_type=f32)
    wide_w = lax.broadcasted_iota(jnp.int32, wide.shape, 0) % levels_w
    wide_n = lax.broadcasted_iota(jnp.int32, wide.shape, 1) // levels_a
    wide = jnp.where(wide_w == wide_n, wide, 0.0).astype(bf16)
    table_rows = levels_e * bands
    into = lax.broadcasted_iota(jnp.int32, (3 * table_rows, wide.shape[0]), 0)
    source = lax.broadcasted_iota(jnp.int32, (3 * table_rows, wide.shape[0]), 1) // levels_w
    within = into % table_rows
    wanted = into - within + (within % bands) * levels_e + within // bands
    lut = jnp.dot(
        jnp.where(source == wanted, 1.0, 0.0).astype(bf16), wide, preferred_element_type=f32
    ).astype(bf16)

    for load in loads[6:]:
        load.wait()
    for w in range(levels_w):
        weights[w] = jnp.maximum(0.0, 1.0 - jnp.abs(vapour_ref[...] - float(w)))
    heights[...] = class_ref[...].astype(f32) + frac_ref[...]

    def smooth(chunk):
        for number, (da, dc, _, _, needed) in enumerate(copies):
            if needed == chunk:

                @pl.when(both(along - da, n_along, across - dc, n_across))
                def _():
                    halo_copy(number).wait_recv()

        fresh = slice(chunk * width + 2 * LANES if chunk else 0, (chunk + 1) * width + 2 * LANES)
        for field in range(2):
            product = jnp.dot(down, padded[field, :, fresh], preferred_element_type=f32)
            high, low = split(product[:rows] + product[rows:])
            tall_high[field * rows : (field + 1) * rows, fresh] = high
            tall_low[field * rows : (field + 1) * rows, fresh] = low
        window = slice(chunk * width, chunk * width + width + 2 * LANES)
        smoothed = dot_nt(tall_high[:, window], across_high)
        smoothed += dot_nt(tall_low[:, window], across_high)
        smoothed += dot_nt(tall_high[:, window], across_low)
        aerosol = smoothed[:rows] / jnp.maximum(smoothed[rows:], 1.0)
        pos_ref[:, chunk * width : (chunk + 1) * width] = (levels_a - 1) * jax.nn.sigmoid(aerosol)

    chosen = []
    for number, side in enumerate(SIDES):
        rank = jnp.int32(0)
        first = [jnp.int32(0) for _ in range(CAP)]
        for s in range(seg_dev):
            hit = routes_ref[1, s] - along == side
            for k in range(CAP):
                first[k] = jnp.where(hit & (rank == k), s, first[k])
            rank = rank + jnp.where(hit, 1, 0)
        chosen.append(first)

    node_a = lax.broadcasted_iota(jnp.int32, (levels_a, width), 0).astype(f32)
    sub = lax.broadcasted_iota(jnp.int32, (8, width), 0)
    lower = sub < bands
    pair_e = (sub // bands).astype(f32)
    per_tile = 8 // bands
    quad = 16 // bands
    group = max(1, 256 // width)

    def correct(chunk, seg):
        at_cols = slice(chunk * width, (chunk + 1) * width)
        base = pl.multiple_of(seg * SEG, SEG)
        base_flat = pl.multiple_of(seg * seg_rows, seg_rows)
        position = pos_ref[pl.ds(base, SEG), at_cols]
        height_rows = heights[pl.ds(base, SEG), at_cols]
        for first in range(0, SEG, quad):
            partial = []
            values = []
            for start in range(first, first + quad, group):
                joints = []
                for row in range(start, start + group):
                    weight_a = jnp.maximum(0.0, 1.0 - jnp.abs(position[row : row + 1] - node_a))
                    joints.append(
                        jnp.concatenate(
                            [
                                (weight_a * weights[w, pl.ds(base + row, 1), at_cols]).astype(bf16)
                                for w in range(levels_w)
                            ],
                            axis=0,
                        )
                    )
                joint = joints[0] if group == 1 else jnp.concatenate(joints, axis=1)
                product = jnp.dot(lut, joint, preferred_element_type=f32)
                for k in range(group):
                    values.append(product[:, k * width : (k + 1) * width])
            for row in range(first, first + quad):
                nodes = values[row - first]
                height = height_rows[row : row + 1]
                sums = [None] * 3
                for k in range(table_rows // 8):
                    weight_e = jnp.maximum(
                        0.0, 1.0 - jnp.abs(height - (pair_e + float(per_tile * k)))
                    )
                    for t in range(3):
                        at = t * table_rows + k * 8
                        term = nodes[at : at + 8] * weight_e
                        sums[t] = term if sums[t] is None else sums[t] + term
                partial.append(sums)
            radiance = toa_ref[pl.ds(base_flat + first * bands, quad * bands), at_cols].astype(f32)
            surfaces = []
            for part in range(quad // 2):
                coefficient = []
                for t in range(3):
                    one, two = partial[2 * part][t], partial[2 * part + 1][t]
                    kept = jnp.where(lower, one, two)
                    moved = pltpu.roll(jnp.where(lower, two, one), bands, 0)
                    coefficient.append(kept + moved)
                scaled = coefficient[0] * radiance[part * 8 : part * 8 + 8] - coefficient[1]
                surfaces.append(scaled / (1.0 + coefficient[2] * scaled))
            corrected[chunk, seg, first * bands : (first + quad) * bands, :] = jnp.concatenate(
                surfaces, axis=0
            ).astype(bf16)

    def correct_from(chunk, low, high):
        def step(seg, carry):
            correct(chunk, seg)
            return carry

        lax.fori_loop(low, high, step, 0)

    def start_slots(chunk):
        for number in order:

            @pl.when(exists(along + SIDES[number], n_along))
            def _():
                slot_copy(chunk, number).start()

    def placed(target):
        row = lax.broadcasted_iota(jnp.int32, (rows * bands, target.shape[1]), 0).astype(f32)
        return jnp.where(row == target, 1.0, 0.0)

    for chunk in range(chunks):
        smooth(chunk)
        if chunk:
            start_slots(chunk - 1)
        correct_from(chunk, 0, seg_dev)
        for number in range(len(SIDES)):
            for k in range(CAP):
                slots[chunk, number * CAP + k] = corrected[chunk, chosen[number][k]]

    lane = lax.broadcasted_iota(jnp.int32, (1, seg_dev * seg_rows), 1)
    target = jnp.full((1, seg_dev * seg_rows), -1, jnp.int32)
    for s in range(seg_dev):
        inside = (lane >= s * seg_rows) & (lane < (s + 1) * seg_rows)
        inside = inside & (routes_ref[0, s] == along)
        target = jnp.where(inside, starts_ref[0, s] * bands + lane - s * seg_rows, target)
    own = placed(target.astype(f32))
    start_slots(chunks - 1)
    count = jnp.sum(own, axis=1, keepdims=True)
    own = own.astype(bf16)
    matrices = {}
    for number in order:

        @pl.when(exists(along - SIDES[number], n_along))
        def _():
            tag_copy(number).wait_recv()

        matrix = placed(got_tags[number, 0:1, :])
        count = count + jnp.sum(matrix, axis=1, keepdims=True)
        matrices[number] = matrix.astype(bf16)
    count = jnp.maximum(count, 1.0)
    for chunk in range(chunks):
        summed = jnp.dot(
            own, corrected[chunk].reshape(seg_dev * seg_rows, width), preferred_element_type=f32
        )
        for number in order:

            @pl.when(exists(along - SIDES[number], n_along))
            def _():
                slot_copy(chunk, number).wait_recv()

            summed = summed + jnp.dot(
                matrices[number],
                got_rows[chunk, number].reshape(CAP * seg_rows, width),
                preferred_element_type=f32,
            )
        result = (summed / count).reshape(rows, bands, width)
        out_ref[:, :, chunk * width : (chunk + 1) * width] = result.astype(bf16)
    for number, (da, dc, _, _, _) in enumerate(copies):

        @pl.when(both(along + da, n_along, across + dc, n_across))
        def _():
            halo_copy(number).wait_send()

    for number in order:

        @pl.when(exists(along + SIDES[number], n_along))
        def _():
            tag_copy(number).wait_send()
            for chunk in range(chunks):
                slot_copy(chunk, number).wait_send()


def body(
    n_along,
    n_across,
    toa_bands,
    dark_mask,
    vapour,
    elev_class,
    elev_frac,
    kernel,
    lut_gain,
    lut_path,
    lut_albedo,
    routes,
    starts,
):
    rows, bands, cols = toa_bands.shape
    half = kernel.shape[0] // 2
    halo = -(-half // 16) * 16
    levels = lut_gain.shape[1:]
    levels_e, levels_a, levels_w = levels
    seg_dev = routes.shape[0]
    seg_rows = SEG * bands
    side_count = len(SIDES)
    width = math.gcd(cols, WIDTH)
    chunks = cols // width
    vmem = pl.BlockSpec(memory_space=pltpu.VMEM)
    smem = pl.BlockSpec(memory_space=pltpu.SMEM)
    hbm = pl.BlockSpec(memory_space=pltpu.HBM)
    table_shape = (bands * levels_e * levels_w, levels_a)
    dma = pltpu.SemaphoreType.DMA

    def table(lut):
        return lut.transpose(0, 1, 3, 2).reshape(table_shape)

    out = pl.pallas_call(
        functools.partial(main_kernel, n_along, n_across, bands, levels),
        out_shape=jax.ShapeDtypeStruct((rows, bands, cols), bf16),
        in_specs=[smem, smem] + [hbm] * 9,
        out_specs=vmem,
        scratch_shapes=[
            pltpu.VMEM((rows, bands, cols), bf16),
            pltpu.VMEM((rows, cols), jnp.int32),
            pltpu.VMEM((1, kernel.shape[0]), f32),
            pltpu.VMEM(table_shape, bf16),
            pltpu.VMEM(table_shape, bf16),
            pltpu.VMEM(table_shape, bf16),
            pltpu.VMEM((rows, cols), f32),
            pltpu.VMEM((rows, cols), jnp.int32),
            pltpu.VMEM((rows, cols), f32),
            pltpu.VMEM((rows * bands, cols), bf16),
            pltpu.VMEM((2, rows, cols), bf16),
            pltpu.VMEM((side_count, 8, CAP * seg_rows), f32),
            pltpu.VMEM((8, LANES), f32),
            pltpu.VMEM((2, rows + 2 * halo, cols + 2 * LANES), bf16),
            pltpu.VMEM((2 * rows, cols + 2 * LANES), bf16),
            pltpu.VMEM((2 * rows, cols + 2 * LANES), bf16),
            pltpu.VMEM((rows, cols), f32),
            pltpu.VMEM((levels_w, rows, cols), f32),
            pltpu.VMEM((rows, cols), f32),
            pltpu.VMEM((chunks, seg_dev, seg_rows, width), bf16),
            pltpu.VMEM((chunks, side_count * CAP, seg_rows, width), bf16),
            pltpu.VMEM((chunks, side_count, CAP, seg_rows, width), bf16),
            pltpu.VMEM((side_count, 8, CAP * seg_rows), f32),
            dma((9,)),
            dma((6 + 2 * chunks,)),
            dma((6 + 2 * chunks,)),
            dma((side_count,)),
            dma((side_count,)),
            dma((chunks, side_count)),
            dma((chunks, side_count)),
        ],
        compiler_params=pltpu.CompilerParams(
            collective_id=0, has_side_effects=True, vmem_limit_bytes=28 * 1024 * 1024
        ),
        name="main",
    )(
        routes.T,
        starts.T,
        *(
            pltpu.with_memory_space_constraint(value, pltpu.HBM)
            for value in (
                toa_bands,
                dark_mask,
                kernel[None],
                table(lut_gain),
                table(lut_path),
                table(lut_albedo),
                vapour,
                elev_class,
                elev_frac,
            )
        ),
    )
    return out[None]


def solution(mesh):
    in_specs = (
        P(("groups", "along"), None, "across"),
        P(("groups", "along"), "across"),
        P(("groups", "along"), "across"),
        P(("groups", "along"), "across"),
        P(("groups", "along"), "across"),
        P(),
        P(),
        P(),
        P(),
        P(("groups", "along"), None),
        P(("groups", "along"), None),
    )
    out_specs = P(("groups", "along"), None, None, "across")
    run = functools.partial(body, mesh.shape["along"], mesh.shape["across"])
    return jax.shard_map(run, mesh=mesh, in_specs=in_specs, out_specs=out_specs, check_vma=False)
```

```python
import functools
import math

import jax
import jax.numpy as jnp
from jax import lax
from jax.experimental import pallas as pl
from jax.experimental.pallas import tpu as pltpu
from jax.sharding import PartitionSpec as P

SEG = 16
REACH = 2
CAP = 2
LANES = 128
WIDTH = 128
MESH_ID = pl.DeviceIdType.MESH
SIDES = [side - REACH for side in range(REACH)] + [side + 1 for side in range(REACH)]
DIRECTIONS = [(da, dc) for da in (-1, 0, 1) for dc in (-1, 0, 1) if (da, dc) != (0, 0)]
f32 = jnp.float32
bf16 = jnp.bfloat16


def split(value):
    high = value.astype(bf16)
    return high, (value - high.astype(f32)).astype(bf16)


def toeplitz(taps, row_count, width, first):
    line = jnp.broadcast_to(taps, (8, taps.shape[1]))
    if width > taps.shape[1]:
        line = jnp.concatenate([line, jnp.zeros((8, width - taps.shape[1]), f32)], axis=1)
    stair = pltpu.roll(line, 0, 1, stride=1, stride_axis=0)
    return jnp.concatenate(
        [pltpu.roll(stair, first + 8 * group, 1) for group in range(row_count // 8)], axis=0
    )


def dot_nt(left, right):
    return lax.dot_general(left, right, (((1,), (1,)), ((), ())), preferred_element_type=f32)


def exists(position, count):
    return (position >= 0) & (position < count)


def both(position_a, count_a, position_c, count_c):
    return exists(position_a, count_a) & exists(position_c, count_c)


def main_kernel(
    n_along,
    n_across,
    bands,
    levels,
    routes_hbm,
    starts_hbm,
    toa_hbm,
    mask_hbm,
    taps_hbm,
    gain_hbm,
    path_hbm,
    albedo_hbm,
    vapour_hbm,
    class_hbm,
    frac_hbm,
    out_ref,
    routes_ref,
    starts_ref,
    raw_ref,
    mask_ref,
    taps_ref,
    gain_ref,
    path_ref,
    albedo_ref,
    vapour_ref,
    class_ref,
    frac_ref,
    toa_ref,
    fields_ref,
    tags_ref,
    taps_pad,
    padded,
    tall_high,
    tall_low,
    pos_ref,
    weights,
    heights,
    corrected,
    slots,
    got_rows,
    got_tags,
    load_sem,
    halo_send,
    halo_recv,
    tag_send,
    tag_recv,
    slot_send,
    slot_recv,
):
    along, across = lax.axis_index("along"), lax.axis_index("across")
    levels_e, levels_a, levels_w = levels
    rows, _, cols = toa_hbm.shape
    halo = (padded.shape[1] - rows) // 2
    half = taps_hbm.shape[1] // 2
    chunks, seg_dev, seg_rows, width = corrected.shape
    loads = [
        pltpu.make_async_copy(source, target, load_sem.at[number])
        for number, (source, target) in enumerate(
            (
                (toa_hbm, raw_ref),
                (mask_hbm, mask_ref),
                (taps_hbm, taps_ref),
                (gain_hbm, gain_ref),
                (path_hbm, path_ref),
                (albedo_hbm, albedo_ref),
                (vapour_hbm, vapour_ref),
                (class_hbm, class_ref),
                (frac_hbm, frac_ref),
                (routes_hbm, routes_ref),
                (starts_hbm, starts_ref),
            )
        )
    ]
    for load in loads:
        load.start()
    barrier = pltpu.get_barrier_semaphore()
    peers = DIRECTIONS + [(side, 0) for side in SIDES if (side, 0) not in DIRECTIONS]
    for da, dc in peers:

        @pl.when(both(along + da, n_along, across + dc, n_across))
        def _():
            pl.semaphore_signal(
                barrier,
                inc=1,
                device_id={"along": along + da, "across": across + dc},
                device_id_type=MESH_ID,
            )

    for load in loads[:2]:
        load.wait()
    flat = raw_ref[...].astype(f32).reshape(rows * bands, cols).astype(bf16)
    row = lax.broadcasted_iota(jnp.int32, (rows, rows * bands), 0) * bands
    col = lax.broadcasted_iota(jnp.int32, (rows, rows * bands), 1)
    pick = jnp.where(col == row, 8.0, 0.0) + jnp.where(col == row + 2, -4.0, 0.0)
    darkness = mask_ref[...].astype(f32)
    value = jnp.dot(pick.astype(bf16), flat, preferred_element_type=f32)
    fields_ref[0] = (darkness * value).astype(bf16)
    fields_ref[1] = darkness.astype(bf16)
    padded[:, halo : halo + rows, LANES : LANES + cols] = fields_ref[...]
    for load in loads[9:]:
        load.wait()
    lane = lax.broadcasted_iota(jnp.int32, (8, CAP * seg_rows), 1)
    for number, side in enumerate(SIDES):
        target = jnp.full((8, CAP * seg_rows), -1, jnp.int32)
        rank = jnp.int32(0)
        for s in range(seg_dev):
            hit = routes_ref[1, s] - along == side
            place = jnp.where(hit, rank, -1)
            inside = (lane >= place * seg_rows) & (lane < (place + 1) * seg_rows) & (place >= 0)
            target = jnp.where(inside, starts_ref[1, s] * bands + lane - place * seg_rows, target)
            rank = rank + jnp.where(hit, 1, 0)
        tags_ref[number] = target.astype(f32)
    spans = {
        -1: (slice(0, halo), slice(halo + rows, 2 * halo + rows)),
        0: (slice(0, rows), slice(halo, halo + rows)),
        1: (slice(rows - halo, rows), slice(0, halo)),
    }
    lanes = {
        -1: (slice(0, LANES), slice(LANES + cols, 2 * LANES + cols)),
        0: (slice(0, cols), slice(LANES, LANES + cols)),
        1: (slice(cols - LANES, cols), slice(0, LANES)),
    }

    copies = []
    for da, dc in DIRECTIONS:
        if dc:
            copies.append((da, dc, lanes[dc][0], lanes[dc][1], 0 if dc > 0 else chunks - 1))
    begin = 0
    for chunk in range(chunks):
        end = min(cols, (chunk + 1) * width + LANES)
        if end > begin:
            for da in (-1, 1):
                copies.append(
                    (da, 0, slice(begin, end), slice(LANES + begin, LANES + end), chunk)
                )
        begin = end

    def halo_copy(number):
        da, dc, source, target, _ = copies[number]
        return pltpu.make_async_remote_copy(
            src_ref=fields_ref.at[:, spans[da][0], source],
            dst_ref=padded.at[:, spans[da][1], target],
            send_sem=halo_send.at[number],
            recv_sem=halo_recv.at[number],
            device_id={"along": along + da, "across": across + dc},
            device_id_type=MESH_ID,
        )

    def tag_copy(number):
        return pltpu.make_async_remote_copy(
            src_ref=tags_ref.at[number],
            dst_ref=got_tags.at[number],
            send_sem=tag_send.at[number],
            recv_sem=tag_recv.at[number],
            device_id={"along": along + SIDES[number]},
            device_id_type=MESH_ID,
        )

    def slot_copy(chunk, number):
        return pltpu.make_async_remote_copy(
            src_ref=slots.at[chunk, pl.ds(number * CAP, CAP)],
            dst_ref=got_rows.at[chunk, number],
            send_sem=slot_send.at[chunk, number],
            recv_sem=slot_recv.at[chunk, number],
            device_id={"along": along + SIDES[number]},
            device_id_type=MESH_ID,
        )

    pl.semaphore_wait(
        barrier,
        sum(
            both(along + da, n_along, across + dc, n_across).astype(jnp.int32) for da, dc in peers
        ),
    )
    for number, (da, dc, _, _, _) in enumerate(copies):

        @pl.when(both(along + da, n_along, across + dc, n_across))
        def _():
            halo_copy(number).start()

    order = sorted(range(len(SIDES)), key=lambda number: abs(SIDES[number]))
    for number in order:

        @pl.when(exists(along + SIDES[number], n_along))
        def _():
            tag_copy(number).start()

        @pl.when(jnp.logical_not(exists(along - SIDES[number], n_along)))
        def _():
            got_rows[:, number] = jnp.zeros((chunks, CAP, seg_rows, width), bf16)
            got_tags[number] = jnp.full(got_tags.shape[1:], -1.0, f32)

    toa_ref[...] = flat
    for da, dc in DIRECTIONS:

        @pl.when(jnp.logical_not(both(along - da, n_along, across - dc, n_across)))
        def _():
            target = padded.at[:, spans[da][1], lanes[dc][1]]
            target[...] = jnp.zeros(target.shape, bf16)

    for load in loads[2:6]:
        load.wait()
    taps_pad[...] = jnp.zeros(taps_pad.shape, f32)
    taps_pad[0:1, 0 : taps_ref.shape[1]] = taps_ref[...]
    taps = taps_pad[0:1, :]
    down_high, down_low = split(toeplitz(taps, rows, 2 * halo + rows, halo - half))
    down = jnp.concatenate([down_high, down_low], axis=0)
    block = width
    across_high, across_low = split(toeplitz(taps, block, block + 2 * LANES, LANES - half))

    node_count = levels_w * levels_a
    tables = jnp.concatenate([gain_ref[...], path_ref[...], albedo_ref[...]], axis=0)
    spread_a = lax.broadcasted_iota(jnp.int32, (levels_a, node_count), 0)
    spread_n = lax.broadcasted_iota(jnp.int32, (levels_a, node_count), 1)
    spread = jnp.where(spread_n % levels_a == spread_a, 1.0, 0.0).astype(bf16)
    wide = jnp.dot(tables, spread, preferred_element_type=f32)
    wide_w = lax.broadcasted_iota(jnp.int32, wide.shape, 0) % levels_w
    wide_n = lax.broadcasted_iota(jnp.int32, wide.shape, 1) // levels_a
    wide = jnp.where(wide_w == wide_n, wide, 0.0).astype(bf16)
    table_rows = levels_e * bands
    into = lax.broadcasted_iota(jnp.int32, (3 * table_rows, wide.shape[0]), 0)
    source = lax.broadcasted_iota(jnp.int32, (3 * table_rows, wide.shape[0]), 1) // levels_w
    within = into % table_rows
    wanted = into - within + (within % bands) * levels_e + within // bands
    lut = jnp.dot(
        jnp.where(source == wanted, 1.0, 0.0).astype(bf16), wide, preferred_element_type=f32
    ).astype(bf16)

    for load in loads[6:9]:
        load.wait()
    for w in range(levels_w):
        weight_w = jnp.maximum(0.0, 1.0 - jnp.abs(vapour_ref[...] - float(w)))
        weights[w] = weight_w.reshape(seg_dev, SEG, cols)
    heights[...] = class_ref[...].astype(f32) + frac_ref[...]

    def smooth(chunk):
        for number, (da, dc, _, _, needed) in enumerate(copies):
            if needed == chunk:

                @pl.when(both(along - da, n_along, across - dc, n_across))
                def _():
                    halo_copy(number).wait_recv()

        fresh = slice(chunk * width + 2 * LANES if chunk else 0, (chunk + 1) * width + 2 * LANES)
        for field in range(2):
            product = jnp.dot(down, padded[field, :, fresh], preferred_element_type=f32)
            high, low = split(product[:rows] + product[rows:])
            tall_high[field * rows : (field + 1) * rows, fresh] = high
            tall_low[field * rows : (field + 1) * rows, fresh] = low
        window = slice(chunk * width, chunk * width + width + 2 * LANES)
        smoothed = dot_nt(tall_high[:, window], across_high)
        smoothed += dot_nt(tall_low[:, window], across_high)
        smoothed += dot_nt(tall_high[:, window], across_low)
        aerosol = smoothed[:rows] / jnp.maximum(smoothed[rows:], 1.0)
        pos_ref[:, chunk * width : (chunk + 1) * width] = (levels_a - 1) * jax.nn.sigmoid(aerosol)

    chosen = []
    for number, side in enumerate(SIDES):
        rank = jnp.int32(0)
        first = [jnp.int32(0) for _ in range(CAP)]
        for s in range(seg_dev):
            hit = routes_ref[1, s] - along == side
            for k in range(CAP):
                first[k] = jnp.where(hit & (rank == k), s, first[k])
            rank = rank + jnp.where(hit, 1, 0)
        chosen.append(first)

    node_a = lax.broadcasted_iota(jnp.int32, (levels_a, width), 0).astype(f32)
    sub = lax.broadcasted_iota(jnp.int32, (8, width), 0)
    lower = sub < bands
    pair_e = (sub // bands).astype(f32)
    per_tile = 8 // bands
    quad = 16 // bands
    group = max(1, 256 // width)

    def correct(chunk, seg):
        at_cols = slice(chunk * width, (chunk + 1) * width)
        base = pl.multiple_of(seg * SEG, SEG)
        base_flat = pl.multiple_of(seg * seg_rows, seg_rows)
        position = pos_ref[pl.ds(base, SEG), at_cols]
        height_rows = heights[pl.ds(base, SEG), at_cols]
        for first in range(0, SEG, quad):
            partial = []
            values = []
            for start in range(first, first + quad, group):
                joints = []
                for row in range(start, start + group):
                    weight_a = jnp.maximum(0.0, 1.0 - jnp.abs(position[row : row + 1] - node_a))
                    joints.append(
                        jnp.concatenate(
                            [
                                (weight_a * weights[w, seg, row : row + 1, at_cols]).astype(bf16)
                                for w in range(levels_w)
                            ],
                            axis=0,
                        )
                    )
                joint = joints[0] if group == 1 else jnp.concatenate(joints, axis=1)
                product = jnp.dot(lut, joint, preferred_element_type=f32)
                for k in range(group):
                    values.append(product[:, k * width : (k + 1) * width])
            for row in range(first, first + quad):
                nodes = values[row - first]
                height = height_rows[row : row + 1]
                sums = [None] * 3
                for k in range(table_rows // 8):
                    weight_e = jnp.maximum(
                        0.0, 1.0 - jnp.abs(height - (pair_e + float(per_tile * k)))
                    )
                    for t in range(3):
                        at = t * table_rows + k * 8
                        term = nodes[at : at + 8] * weight_e
                        sums[t] = term if sums[t] is None else sums[t] + term
                partial.append(sums)
            radiance = toa_ref[pl.ds(base_flat + first * bands, quad * bands), at_cols].astype(f32)
            surfaces = []
            for part in range(quad // 2):
                coefficient = []
                for t in range(3):
                    one, two = partial[2 * part][t], partial[2 * part + 1][t]
                    kept = jnp.where(lower, one, two)
                    moved = pltpu.roll(jnp.where(lower, two, one), bands, 0)
                    coefficient.append(kept + moved)
                scaled = coefficient[0] * radiance[part * 8 : part * 8 + 8] - coefficient[1]
                surfaces.append(scaled / (1.0 + coefficient[2] * scaled))
            corrected[chunk, seg, first * bands : (first + quad) * bands, :] = jnp.concatenate(
                surfaces, axis=0
            ).astype(bf16)

    def correct_from(chunk, low, high):
        def step(seg, carry):
            correct(chunk, seg)
            return carry

        lax.fori_loop(low, high, step, 0)

    def start_slots(chunk):
        for number in order:

            @pl.when(exists(along + SIDES[number], n_along))
            def _():
                slot_copy(chunk, number).start()

    def placed(target):
        row = lax.broadcasted_iota(jnp.int32, (rows * bands, target.shape[1]), 0).astype(f32)
        return jnp.where(row == target, 1.0, 0.0)

    for chunk in range(chunks):
        smooth(chunk)
        if chunk:
            start_slots(chunk - 1)
        correct_from(chunk, 0, seg_dev)
        for number in range(len(SIDES)):
            for k in range(CAP):
                slots[chunk, number * CAP + k] = corrected[chunk, chosen[number][k]]

    lane = lax.broadcasted_iota(jnp.int32, (1, seg_dev * seg_rows), 1)
    target = jnp.full((1, seg_dev * seg_rows), -1, jnp.int32)
    for s in range(seg_dev):
        inside = (lane >= s * seg_rows) & (lane < (s + 1) * seg_rows)
        inside = inside & (routes_ref[0, s] == along)
        target = jnp.where(inside, starts_ref[0, s] * bands + lane - s * seg_rows, target)
    own = placed(target.astype(f32))
    start_slots(chunks - 1)
    count = jnp.sum(own, axis=1, keepdims=True)
    own = own.astype(bf16)
    matrices = {}
    for number in order:

        @pl.when(exists(along - SIDES[number], n_along))
        def _():
            tag_copy(number).wait_recv()

        matrix = placed(got_tags[number, 0:1, :])
        count = count + jnp.sum(matrix, axis=1, keepdims=True)
        matrices[number] = matrix.astype(bf16)
    count = jnp.maximum(count, 1.0)
    for chunk in range(chunks):
        summed = jnp.dot(
            own, corrected[chunk].reshape(seg_dev * seg_rows, width), preferred_element_type=f32
        )
        for number in order:

            @pl.when(exists(along - SIDES[number], n_along))
            def _():
                slot_copy(chunk, number).wait_recv()

            summed = summed + jnp.dot(
                matrices[number],
                got_rows[chunk, number].reshape(CAP * seg_rows, width),
                preferred_element_type=f32,
            )
        result = (summed / count).reshape(rows, bands, width)
        out_ref[:, :, chunk * width : (chunk + 1) * width] = result.astype(bf16)
    for number, (da, dc, _, _, _) in enumerate(copies):

        @pl.when(both(along + da, n_along, across + dc, n_across))
        def _():
            halo_copy(number).wait_send()

    for number in order:

        @pl.when(exists(along + SIDES[number], n_along))
        def _():
            tag_copy(number).wait_send()
            for chunk in range(chunks):
                slot_copy(chunk, number).wait_send()


def body(
    n_along,
    n_across,
    toa_bands,
    dark_mask,
    vapour,
    elev_class,
    elev_frac,
    kernel,
    lut_gain,
    lut_path,
    lut_albedo,
    routes,
    starts,
):
    rows, bands, cols = toa_bands.shape
    half = kernel.shape[0] // 2
    halo = -(-half // 16) * 16
    levels = lut_gain.shape[1:]
    levels_e, levels_a, levels_w = levels
    seg_dev = routes.shape[0]
    seg_rows = SEG * bands
    side_count = len(SIDES)
    width = math.gcd(cols, WIDTH)
    chunks = cols // width
    vmem = pl.BlockSpec(memory_space=pltpu.VMEM)
    hbm = pl.BlockSpec(memory_space=pltpu.HBM)
    table_shape = (bands * levels_e * levels_w, levels_a)
    dma = pltpu.SemaphoreType.DMA

    def table(lut):
        return lut.transpose(0, 1, 3, 2).reshape(table_shape)

    out = pl.pallas_call(
        functools.partial(main_kernel, n_along, n_across, bands, levels),
        out_shape=jax.ShapeDtypeStruct((rows, bands, cols), bf16),
        in_specs=[hbm] * 11,
        out_specs=vmem,
        scratch_shapes=[
            pltpu.SMEM((2, seg_dev), jnp.int32),
            pltpu.SMEM((2, seg_dev), jnp.int32),
            pltpu.VMEM((rows, bands, cols), bf16),
            pltpu.VMEM((rows, cols), jnp.int32),
            pltpu.VMEM((1, kernel.shape[0]), f32),
            pltpu.VMEM(table_shape, bf16),
            pltpu.VMEM(table_shape, bf16),
            pltpu.VMEM(table_shape, bf16),
            pltpu.VMEM((rows, cols), f32),
            pltpu.VMEM((rows, cols), jnp.int32),
            pltpu.VMEM((rows, cols), f32),
            pltpu.VMEM((rows * bands, cols), bf16),
            pltpu.VMEM((2, rows, cols), bf16),
            pltpu.VMEM((side_count, 8, CAP * seg_rows), f32),
            pltpu.VMEM((8, LANES), f32),
            pltpu.VMEM((2, rows + 2 * halo, cols + 2 * LANES), bf16),
            pltpu.VMEM((2 * rows, cols + 2 * LANES), bf16),
            pltpu.VMEM((2 * rows, cols + 2 * LANES), bf16),
            pltpu.VMEM((rows, cols), f32),
            pltpu.VMEM((levels_w, seg_dev, SEG, cols), f32),
            pltpu.VMEM((rows, cols), f32),
            pltpu.VMEM((chunks, seg_dev, seg_rows, width), bf16),
            pltpu.VMEM((chunks, side_count * CAP, seg_rows, width), bf16),
            pltpu.VMEM((chunks, side_count, CAP, seg_rows, width), bf16),
            pltpu.VMEM((side_count, 8, CAP * seg_rows), f32),
            dma((11,)),
            dma((6 + 2 * chunks,)),
            dma((6 + 2 * chunks,)),
            dma((side_count,)),
            dma((side_count,)),
            dma((chunks, side_count)),
            dma((chunks, side_count)),
        ],
        compiler_params=pltpu.CompilerParams(
            collective_id=0, has_side_effects=True, vmem_limit_bytes=28 * 1024 * 1024
        ),
        name="main",
    )(
        *(
            pltpu.with_memory_space_constraint(value, pltpu.HBM)
            for value in (
                routes.T,
                starts.T,
                toa_bands,
                dark_mask,
                kernel[None],
                table(lut_gain),
                table(lut_path),
                table(lut_albedo),
                vapour,
                elev_class,
                elev_frac,
            )
        ),
    )
    return out[None]


def solution(mesh):
    in_specs = (
        P(("groups", "along"), None, "across"),
        P(("groups", "along"), "across"),
        P(("groups", "along"), "across"),
        P(("groups", "along"), "across"),
        P(("groups", "along"), "across"),
        P(),
        P(),
        P(),
        P(),
        P(("groups", "along"), None),
        P(("groups", "along"), None),
    )
    out_specs = P(("groups", "along"), None, None, "across")
    run = functools.partial(body, mesh.shape["along"], mesh.shape["across"])
    return jax.shard_map(run, mesh=mesh, in_specs=in_specs, out_specs=out_specs, check_vma=False)
```

```python
import functools
import math

import jax
import jax.numpy as jnp
from jax import lax
from jax.experimental import pallas as pl
from jax.experimental.pallas import tpu as pltpu
from jax.sharding import PartitionSpec as P

SEG = 16
REACH = 2
CAP = 2
LANES = 128
WIDTH = 128
MESH_ID = pl.DeviceIdType.MESH
SIDES = [side - REACH for side in range(REACH)] + [side + 1 for side in range(REACH)]
DIRECTIONS = [(da, dc) for da in (-1, 0, 1) for dc in (-1, 0, 1) if (da, dc) != (0, 0)]
f32 = jnp.float32
bf16 = jnp.bfloat16


def split(value):
    high = value.astype(bf16)
    return high, (value - high.astype(f32)).astype(bf16)


def toeplitz(taps, row_count, width, first):
    line = jnp.broadcast_to(taps, (8, taps.shape[1]))
    if width > taps.shape[1]:
        line = jnp.concatenate([line, jnp.zeros((8, width - taps.shape[1]), f32)], axis=1)
    stair = pltpu.roll(line, 0, 1, stride=1, stride_axis=0)
    return jnp.concatenate(
        [pltpu.roll(stair, first + 8 * group, 1) for group in range(row_count // 8)], axis=0
    )


def dot_nt(left, right):
    return lax.dot_general(left, right, (((1,), (1,)), ((), ())), preferred_element_type=f32)


def exists(position, count):
    return (position >= 0) & (position < count)


def both(position_a, count_a, position_c, count_c):
    return exists(position_a, count_a) & exists(position_c, count_c)


def main_kernel(
    n_along,
    n_across,
    bands,
    levels,
    routes_hbm,
    starts_hbm,
    toa_hbm,
    mask_hbm,
    taps_hbm,
    gain_hbm,
    path_hbm,
    albedo_hbm,
    vapour_hbm,
    class_hbm,
    frac_hbm,
    out_ref,
    routes_ref,
    starts_ref,
    raw_ref,
    mask_ref,
    taps_ref,
    gain_ref,
    path_ref,
    albedo_ref,
    vapour_ref,
    class_ref,
    frac_ref,
    toa_ref,
    fields_ref,
    tags_ref,
    taps_pad,
    padded,
    tall_high,
    tall_low,
    pos_ref,
    weights,
    heights,
    corrected,
    slots,
    got_rows,
    got_tags,
    load_sem,
    halo_send,
    halo_recv,
    tag_send,
    tag_recv,
    slot_send,
    slot_recv,
):
    along, across = lax.axis_index("along"), lax.axis_index("across")
    levels_e, levels_a, levels_w = levels
    rows, _, cols = toa_hbm.shape
    halo = (padded.shape[1] - rows) // 2
    half = taps_hbm.shape[1] // 2
    chunks, seg_dev, seg_rows, width = corrected.shape
    loads = [
        pltpu.make_async_copy(source, target, load_sem.at[number])
        for number, (source, target) in enumerate(
            (
                (toa_hbm, raw_ref),
                (mask_hbm, mask_ref),
                (taps_hbm, taps_ref),
                (gain_hbm, gain_ref),
                (path_hbm, path_ref),
                (albedo_hbm, albedo_ref),
                (vapour_hbm, vapour_ref),
                (class_hbm, class_ref),
                (frac_hbm, frac_ref),
                (routes_hbm, routes_ref),
                (starts_hbm, starts_ref),
            )
        )
    ]
    for load in loads[:2]:
        load.start()
    barrier = pltpu.get_barrier_semaphore()
    peers = DIRECTIONS + [(side, 0) for side in SIDES if (side, 0) not in DIRECTIONS]
    for da, dc in peers:

        @pl.when(both(along + da, n_along, across + dc, n_across))
        def _():
            pl.semaphore_signal(
                barrier,
                inc=1,
                device_id={"along": along + da, "across": across + dc},
                device_id_type=MESH_ID,
            )

    row = lax.broadcasted_iota(jnp.int32, (rows, rows * bands), 0) * bands
    col = lax.broadcasted_iota(jnp.int32, (rows, rows * bands), 1)
    pick = jnp.where(col == row, 8.0, 0.0) + jnp.where(col == row + 2, -4.0, 0.0)
    for load in loads[:2]:
        load.wait()
    for load in loads[2:]:
        load.start()
    flat = raw_ref[...].astype(f32).reshape(rows * bands, cols).astype(bf16)
    darkness = mask_ref[...].astype(f32)
    value = jnp.dot(pick.astype(bf16), flat, preferred_element_type=f32)
    fields_ref[0] = (darkness * value).astype(bf16)
    fields_ref[1] = darkness.astype(bf16)
    spans = {
        -1: (slice(0, halo), slice(halo + rows, 2 * halo + rows)),
        0: (slice(0, rows), slice(halo, halo + rows)),
        1: (slice(rows - halo, rows), slice(0, halo)),
    }
    lanes = {
        -1: (slice(0, LANES), slice(LANES + cols, 2 * LANES + cols)),
        0: (slice(0, cols), slice(LANES, LANES + cols)),
        1: (slice(cols - LANES, cols), slice(0, LANES)),
    }

    copies = []
    for da, dc in DIRECTIONS:
        if dc:
            copies.append((da, dc, lanes[dc][0], lanes[dc][1], 0 if dc > 0 else chunks - 1))
    begin = 0
    for chunk in range(chunks):
        end = min(cols, (chunk + 1) * width + LANES)
        if end > begin:
            for da in (-1, 1):
                copies.append(
                    (da, 0, slice(begin, end), slice(LANES + begin, LANES + end), chunk)
                )
        begin = end

    def halo_copy(number):
        da, dc, source, target, _ = copies[number]
        return pltpu.make_async_remote_copy(
            src_ref=fields_ref.at[:, spans[da][0], source],
            dst_ref=padded.at[:, spans[da][1], target],
            send_sem=halo_send.at[number],
            recv_sem=halo_recv.at[number],
            device_id={"along": along + da, "across": across + dc},
            device_id_type=MESH_ID,
        )

    def tag_copy(number):
        return pltpu.make_async_remote_copy(
            src_ref=tags_ref.at[number],
            dst_ref=got_tags.at[number],
            send_sem=tag_send.at[number],
            recv_sem=tag_recv.at[number],
            device_id={"along": along + SIDES[number]},
            device_id_type=MESH_ID,
        )

    def slot_copy(chunk, number):
        return pltpu.make_async_remote_copy(
            src_ref=slots.at[chunk, pl.ds(number * CAP, CAP)],
            dst_ref=got_rows.at[chunk, number],
            send_sem=slot_send.at[chunk, number],
            recv_sem=slot_recv.at[chunk, number],
            device_id={"along": along + SIDES[number]},
            device_id_type=MESH_ID,
        )

    pl.semaphore_wait(
        barrier,
        sum(
            both(along + da, n_along, across + dc, n_across).astype(jnp.int32) for da, dc in peers
        ),
    )
    for number, (da, dc, _, _, _) in enumerate(copies):

        @pl.when(both(along + da, n_along, across + dc, n_across))
        def _():
            halo_copy(number).start()

    padded[:, halo : halo + rows, LANES : LANES + cols] = fields_ref[...]
    for load in loads[9:]:
        load.wait()
    lane = lax.broadcasted_iota(jnp.int32, (8, CAP * seg_rows), 1)
    for number, side in enumerate(SIDES):
        target = jnp.full((8, CAP * seg_rows), -1, jnp.int32)
        rank = jnp.int32(0)
        for s in range(seg_dev):
            hit = routes_ref[1, s] - along == side
            place = jnp.where(hit, rank, -1)
            inside = (lane >= place * seg_rows) & (lane < (place + 1) * seg_rows) & (place >= 0)
            target = jnp.where(inside, starts_ref[1, s] * bands + lane - place * seg_rows, target)
            rank = rank + jnp.where(hit, 1, 0)
        tags_ref[number] = target.astype(f32)
    order = sorted(range(len(SIDES)), key=lambda number: abs(SIDES[number]))
    for number in order:

        @pl.when(exists(along + SIDES[number], n_along))
        def _():
            tag_copy(number).start()

        @pl.when(jnp.logical_not(exists(along - SIDES[number], n_along)))
        def _():
            got_rows[:, number] = jnp.zeros((chunks, CAP, seg_rows, width), bf16)
            got_tags[number] = jnp.full(got_tags.shape[1:], -1.0, f32)

    toa_ref[...] = flat
    for da, dc in DIRECTIONS:

        @pl.when(jnp.logical_not(both(along - da, n_along, across - dc, n_across)))
        def _():
            target = padded.at[:, spans[da][1], lanes[dc][1]]
            target[...] = jnp.zeros(target.shape, bf16)

    for load in loads[2:6]:
        load.wait()
    taps_pad[...] = jnp.zeros(taps_pad.shape, f32)
    taps_pad[0:1, 0 : taps_ref.shape[1]] = taps_ref[...]
    taps = taps_pad[0:1, :]
    down_high, down_low = split(toeplitz(taps, rows, 2 * halo + rows, halo - half))
    down = jnp.concatenate([down_high, down_low], axis=0)
    block = width
    across_high, across_low = split(toeplitz(taps, block, block + 2 * LANES, LANES - half))

    node_count = levels_w * levels_a
    tables = jnp.concatenate([gain_ref[...], path_ref[...], albedo_ref[...]], axis=0)
    spread_a = lax.broadcasted_iota(jnp.int32, (levels_a, node_count), 0)
    spread_n = lax.broadcasted_iota(jnp.int32, (levels_a, node_count), 1)
    spread = jnp.where(spread_n % levels_a == spread_a, 1.0, 0.0).astype(bf16)
    wide = jnp.dot(tables, spread, preferred_element_type=f32)
    wide_w = lax.broadcasted_iota(jnp.int32, wide.shape, 0) % levels_w
    wide_n = lax.broadcasted_iota(jnp.int32, wide.shape, 1) // levels_a
    wide = jnp.where(wide_w == wide_n, wide, 0.0).astype(bf16)
    table_rows = levels_e * bands
    into = lax.broadcasted_iota(jnp.int32, (3 * table_rows, wide.shape[0]), 0)
    source = lax.broadcasted_iota(jnp.int32, (3 * table_rows, wide.shape[0]), 1) // levels_w
    within = into % table_rows
    wanted = into - within + (within % bands) * levels_e + within // bands
    lut = jnp.dot(
        jnp.where(source == wanted, 1.0, 0.0).astype(bf16), wide, preferred_element_type=f32
    ).astype(bf16)

    for load in loads[6:9]:
        load.wait()
    for w in range(levels_w):
        weight_w = jnp.maximum(0.0, 1.0 - jnp.abs(vapour_ref[...] - float(w)))
        weights[w] = weight_w.reshape(seg_dev, SEG, cols)
    heights[...] = class_ref[...].astype(f32) + frac_ref[...]

    def smooth(chunk):
        for number, (da, dc, _, _, needed) in enumerate(copies):
            if needed == chunk:

                @pl.when(both(along - da, n_along, across - dc, n_across))
                def _():
                    halo_copy(number).wait_recv()

        fresh = slice(chunk * width + 2 * LANES if chunk else 0, (chunk + 1) * width + 2 * LANES)
        for field in range(2):
            product = jnp.dot(down, padded[field, :, fresh], preferred_element_type=f32)
            high, low = split(product[:rows] + product[rows:])
            tall_high[field * rows : (field + 1) * rows, fresh] = high
            tall_low[field * rows : (field + 1) * rows, fresh] = low
        window = slice(chunk * width, chunk * width + width + 2 * LANES)
        smoothed = dot_nt(tall_high[:, window], across_high)
        smoothed += dot_nt(tall_low[:, window], across_high)
        smoothed += dot_nt(tall_high[:, window], across_low)
        aerosol = smoothed[:rows] / jnp.maximum(smoothed[rows:], 1.0)
        pos_ref[:, chunk * width : (chunk + 1) * width] = (levels_a - 1) * jax.nn.sigmoid(aerosol)

    chosen = []
    for number, side in enumerate(SIDES):
        rank = jnp.int32(0)
        first = [jnp.int32(0) for _ in range(CAP)]
        for s in range(seg_dev):
            hit = routes_ref[1, s] - along == side
            for k in range(CAP):
                first[k] = jnp.where(hit & (rank == k), s, first[k])
            rank = rank + jnp.where(hit, 1, 0)
        chosen.append(first)

    node_a = lax.broadcasted_iota(jnp.int32, (levels_a, width), 0).astype(f32)
    sub = lax.broadcasted_iota(jnp.int32, (8, width), 0)
    lower = sub < bands
    pair_e = (sub // bands).astype(f32)
    per_tile = 8 // bands
    quad = 16 // bands
    group = max(1, 256 // width)

    def correct(chunk, seg):
        at_cols = slice(chunk * width, (chunk + 1) * width)
        base = pl.multiple_of(seg * SEG, SEG)
        base_flat = pl.multiple_of(seg * seg_rows, seg_rows)
        position = pos_ref[pl.ds(base, SEG), at_cols]
        height_rows = heights[pl.ds(base, SEG), at_cols]
        for first in range(0, SEG, quad):
            partial = []
            values = []
            for start in range(first, first + quad, group):
                joints = []
                for row in range(start, start + group):
                    weight_a = jnp.maximum(0.0, 1.0 - jnp.abs(position[row : row + 1] - node_a))
                    joints.append(
                        jnp.concatenate(
                            [
                                (weight_a * weights[w, seg, row : row + 1, at_cols]).astype(bf16)
                                for w in range(levels_w)
                            ],
                            axis=0,
                        )
                    )
                joint = joints[0] if group == 1 else jnp.concatenate(joints, axis=1)
                product = jnp.dot(lut, joint, preferred_element_type=f32)
                for k in range(group):
                    values.append(product[:, k * width : (k + 1) * width])
            for row in range(first, first + quad):
                nodes = values[row - first]
                height = height_rows[row : row + 1]
                sums = [None] * 3
                for k in range(table_rows // 8):
                    weight_e = jnp.maximum(
                        0.0, 1.0 - jnp.abs(height - (pair_e + float(per_tile * k)))
                    )
                    for t in range(3):
                        at = t * table_rows + k * 8
                        term = nodes[at : at + 8] * weight_e
                        sums[t] = term if sums[t] is None else sums[t] + term
                partial.append(sums)
            radiance = toa_ref[pl.ds(base_flat + first * bands, quad * bands), at_cols].astype(f32)
            surfaces = []
            for part in range(quad // 2):
                coefficient = []
                for t in range(3):
                    one, two = partial[2 * part][t], partial[2 * part + 1][t]
                    kept = jnp.where(lower, one, two)
                    moved = pltpu.roll(jnp.where(lower, two, one), bands, 0)
                    coefficient.append(kept + moved)
                scaled = coefficient[0] * radiance[part * 8 : part * 8 + 8] - coefficient[1]
                surfaces.append(scaled / (1.0 + coefficient[2] * scaled))
            corrected[chunk, seg, first * bands : (first + quad) * bands, :] = jnp.concatenate(
                surfaces, axis=0
            ).astype(bf16)

    def correct_from(chunk, low, high):
        def step(seg, carry):
            correct(chunk, seg)
            return carry

        lax.fori_loop(low, high, step, 0)

    def start_slots(chunk):
        for number in order:

            @pl.when(exists(along + SIDES[number], n_along))
            def _():
                slot_copy(chunk, number).start()

    def placed(target):
        row = lax.broadcasted_iota(jnp.int32, (rows * bands, target.shape[1]), 0).astype(f32)
        return jnp.where(row == target, 1.0, 0.0)

    for chunk in range(chunks):
        smooth(chunk)
        if chunk:
            start_slots(chunk - 1)
        correct_from(chunk, 0, seg_dev)
        for number in range(len(SIDES)):
            for k in range(CAP):
                slots[chunk, number * CAP + k] = corrected[chunk, chosen[number][k]]

    lane = lax.broadcasted_iota(jnp.int32, (1, seg_dev * seg_rows), 1)
    target = jnp.full((1, seg_dev * seg_rows), -1, jnp.int32)
    for s in range(seg_dev):
        inside = (lane >= s * seg_rows) & (lane < (s + 1) * seg_rows)
        inside = inside & (routes_ref[0, s] == along)
        target = jnp.where(inside, starts_ref[0, s] * bands + lane - s * seg_rows, target)
    own = placed(target.astype(f32))
    start_slots(chunks - 1)
    count = jnp.sum(own, axis=1, keepdims=True)
    own = own.astype(bf16)
    matrices = {}
    for number in order:

        @pl.when(exists(along - SIDES[number], n_along))
        def _():
            tag_copy(number).wait_recv()

        matrix = placed(got_tags[number, 0:1, :])
        count = count + jnp.sum(matrix, axis=1, keepdims=True)
        matrices[number] = matrix.astype(bf16)
    count = jnp.maximum(count, 1.0)
    for chunk in range(chunks):
        summed = jnp.dot(
            own, corrected[chunk].reshape(seg_dev * seg_rows, width), preferred_element_type=f32
        )
        for number in order:

            @pl.when(exists(along - SIDES[number], n_along))
            def _():
                slot_copy(chunk, number).wait_recv()

            summed = summed + jnp.dot(
                matrices[number],
                got_rows[chunk, number].reshape(CAP * seg_rows, width),
                preferred_element_type=f32,
            )
        result = (summed / count).reshape(rows, bands, width)
        out_ref[:, :, chunk * width : (chunk + 1) * width] = result.astype(bf16)
    for number, (da, dc, _, _, _) in enumerate(copies):

        @pl.when(both(along + da, n_along, across + dc, n_across))
        def _():
            halo_copy(number).wait_send()

    for number in order:

        @pl.when(exists(along + SIDES[number], n_along))
        def _():
            tag_copy(number).wait_send()
            for chunk in range(chunks):
                slot_copy(chunk, number).wait_send()


def body(
    n_along,
    n_across,
    toa_bands,
    dark_mask,
    vapour,
    elev_class,
    elev_frac,
    kernel,
    lut_gain,
    lut_path,
    lut_albedo,
    routes,
    starts,
):
    rows, bands, cols = toa_bands.shape
    half = kernel.shape[0] // 2
    halo = -(-half // 16) * 16
    levels = lut_gain.shape[1:]
    levels_e, levels_a, levels_w = levels
    seg_dev = routes.shape[0]
    seg_rows = SEG * bands
    side_count = len(SIDES)
    width = math.gcd(cols, WIDTH)
    chunks = cols // width
    vmem = pl.BlockSpec(memory_space=pltpu.VMEM)
    hbm = pl.BlockSpec(memory_space=pltpu.HBM)
    table_shape = (bands * levels_e * levels_w, levels_a)
    dma = pltpu.SemaphoreType.DMA

    def table(lut):
        return lut.transpose(0, 1, 3, 2).reshape(table_shape)

    out = pl.pallas_call(
        functools.partial(main_kernel, n_along, n_across, bands, levels),
        out_shape=jax.ShapeDtypeStruct((rows, bands, cols), bf16),
        in_specs=[hbm] * 11,
        out_specs=vmem,
        scratch_shapes=[
            pltpu.SMEM((2, seg_dev), jnp.int32),
            pltpu.SMEM((2, seg_dev), jnp.int32),
            pltpu.VMEM((rows, bands, cols), bf16),
            pltpu.VMEM((rows, cols), jnp.int32),
            pltpu.VMEM((1, kernel.shape[0]), f32),
            pltpu.VMEM(table_shape, bf16),
            pltpu.VMEM(table_shape, bf16),
            pltpu.VMEM(table_shape, bf16),
            pltpu.VMEM((rows, cols), f32),
            pltpu.VMEM((rows, cols), jnp.int32),
            pltpu.VMEM((rows, cols), f32),
            pltpu.VMEM((rows * bands, cols), bf16),
            pltpu.VMEM((2, rows, cols), bf16),
            pltpu.VMEM((side_count, 8, CAP * seg_rows), f32),
            pltpu.VMEM((8, LANES), f32),
            pltpu.VMEM((2, rows + 2 * halo, cols + 2 * LANES), bf16),
            pltpu.VMEM((2 * rows, cols + 2 * LANES), bf16),
            pltpu.VMEM((2 * rows, cols + 2 * LANES), bf16),
            pltpu.VMEM((rows, cols), f32),
            pltpu.VMEM((levels_w, seg_dev, SEG, cols), f32),
            pltpu.VMEM((rows, cols), f32),
            pltpu.VMEM((chunks, seg_dev, seg_rows, width), bf16),
            pltpu.VMEM((chunks, side_count * CAP, seg_rows, width), bf16),
            pltpu.VMEM((chunks, side_count, CAP, seg_rows, width), bf16),
            pltpu.VMEM((side_count, 8, CAP * seg_rows), f32),
            dma((11,)),
            dma((6 + 2 * chunks,)),
            dma((6 + 2 * chunks,)),
            dma((side_count,)),
            dma((side_count,)),
            dma((chunks, side_count)),
            dma((chunks, side_count)),
        ],
        compiler_params=pltpu.CompilerParams(
            collective_id=0, has_side_effects=True, vmem_limit_bytes=28 * 1024 * 1024
        ),
        name="main",
    )(
        *(
            pltpu.with_memory_space_constraint(value, pltpu.HBM)
            for value in (
                routes.T,
                starts.T,
                toa_bands,
                dark_mask,
                kernel[None],
                table(lut_gain),
                table(lut_path),
                table(lut_albedo),
                vapour,
                elev_class,
                elev_frac,
            )
        ),
    )
    return out[None]


def solution(mesh):
    in_specs = (
        P(("groups", "along"), None, "across"),
        P(("groups", "along"), "across"),
        P(("groups", "along"), "across"),
        P(("groups", "along"), "across"),
        P(("groups", "along"), "across"),
        P(),
        P(),
        P(),
        P(),
        P(("groups", "along"), None),
        P(("groups", "along"), None),
    )
    out_specs = P(("groups", "along"), None, None, "across")
    run = functools.partial(body, mesh.shape["along"], mesh.shape["across"])
    return jax.shard_map(run, mesh=mesh, in_specs=in_specs, out_specs=out_specs, check_vma=False)
```
